512 devices in a mesh: seq: 32 (over x, z), exp: 16 (over y, core).
Axes of the slice: x: 4, y: 8, z: 8, core: 2. Of those that a mesh axis runs over, the one named last changes fastest.
Arguments:
- queries: bfloat16 [8192, 2048], P('seq', 'exp'), may hold values from -112 to 112
- key_rows: bfloat16 [8192, 2048], P('seq', 'exp'), may hold values from -4 to 4
- value_rows: bfloat16 [8192, 2048], P('seq', 'exp'), may hold values from -6 to 6
- out_grad: bfloat16 [8192, 2048], P('seq', 'exp'), may hold values from -6 to 6
- expert_ids: int32 [8192, 2], P('seq'), may hold values from 0 to 31, all different within a row
- gate_values: float32 [8192, 2], P('seq'), may hold values from 0.1 to 1
- alibi_slope: float32 [16], P('exp'), may hold values from 0.00012207031 to 0.1
- expert_in: bfloat16 [32, 2048, 4096], P('seq', None, 'exp'), may hold values from -0.125 to 0.125
- expert_out: bfloat16 [32, 4096, 2048], P('seq', 'exp'), may hold values from -0.09375 to 0.09375
Outputs:
- query_grad: bfloat16 [8192, 2048], P('seq', 'exp')
- key_grad: bfloat16 [8192, 2048], P('seq', 'exp')
- value_grad: bfloat16 [8192, 2048], P('seq', 'exp')
- expert_in_grad: bfloat16 [32, 2048, 4096], P('seq', None, 'exp')
- expert_out_grad: bfloat16 [32, 4096, 2048], P('seq', 'exp')
The draws below stay inside these ranges and needn't reach their ends.
Inputs may be any that keep to these rules, and one draw needn't show every extreme that they name: `expert_ids`: each token names two different experts.
All inputs are finite; a program needn't handle non-finite values.
Results may differ from the reference program's by a relative error of at most 0.024.
Values may be sent and summed in bfloat16 or wider, within the bound.
A program may use at most 128 MiB of HBM per device.

```python
import math
import jax
import jax.numpy as jnp
from jax import lax

D = 2048
H = 16
HD = 128
FF = 4096
BLOCK = 256
WCH = 16
EXPERTS = 32
CAP = 20
TOKENS = 8192
N_SEQ = 32
N_EXP = 16


def drawn_pair(key):
    base_keys = jnp.clip(jax.random.normal(jax.random.fold_in(key, 11), (TOKENS, D), jnp.float32), -4.0, 4.0)
    base_queries = jnp.clip(jax.random.normal(jax.random.fold_in(key, 12), (TOKENS, D), jnp.float32), -4.0, 4.0)
    return (base_queries, base_keys)


def draw_queries(key, part):
    return drawn_pair(key)[0].astype(jnp.bfloat16)


def draw_key_rows(key, part):
    return drawn_pair(key)[1].astype(jnp.bfloat16)


def steps_of(rng, dims, pieces, low, high):
    gain, own = 1.0, jax.random.fold_in(rng, 6)
    for axis_at, shards_of in pieces:
        draws = jnp.exp(jax.random.uniform(jax.random.fold_in(own, axis_at), (shards_of,), jnp.float32, low / len(pieces), high / len(pieces)))
        gain = gain * jnp.repeat(draws, dims[axis_at] // shards_of).reshape([-1 if axis == axis_at else 1 for axis in range(len(dims))])
    return gain


def picks_of(stream_key, rows, number_of, top, lift):
    order = jax.random.permutation(jax.random.fold_in(stream_key, 1), number_of)
    pull = order
    for power in range(3):
        pull = pull * pull // number_of
    pull = pull * lift // number_of
    chance = jax.random.randint(jax.random.fold_in(stream_key, 2), (rows, number_of), 0, 4096) + pull
    fixed_rows = jax.random.permutation(jax.random.fold_in(stream_key, 3), rows)[jnp.arange(number_of) % rows]
    chance = jnp.where(jnp.arange(rows)[:, None] == fixed_rows[None, :], 1 << 14, chance)
    priority = chance * number_of + jnp.arange(number_of)
    return lax.top_k(priority.astype(jnp.int32), top)[1].astype(jnp.int32)


def gaussian(stream_key, extent, deviation, limit, shards=(), held_as=jnp.bfloat16):
    array = deviation * jax.random.normal(stream_key, extent, jnp.float32)
    if shards:
        array = array * steps_of(stream_key, extent, shards, -0.22, 0.18)
    return jnp.clip(array, -limit, limit).astype(held_as)


def setup_inputs(seed: int = 0) -> dict:
    seeds = jax.random.split(jax.random.key(seed), 10)
    return {
        "queries": draw_queries(jax.random.fold_in(seeds[9], 71), 0),
        "key_rows": draw_key_rows(jax.random.fold_in(seeds[9], 71), 0),
        "value_rows": gaussian(seeds[2], (TOKENS, D), 1.0, 6.0, ((0, 32), (1, 16))),
        "out_grad": gaussian(seeds[3], (TOKENS, D), 1.0, 6.0, ((0, 32), (1, 16))),
        "expert_ids": picks_of(seeds[4], TOKENS, EXPERTS, 2, 1024),
        "gate_values": jnp.clip(0.1 + 0.9 * jax.random.uniform(seeds[5], (TOKENS, 2), jnp.float32) ** steps_of(seeds[5], (TOKENS, 2), ((0, 32),), -0.2, 0.2), 0.1, 1.0),
        "alibi_slope": jnp.clip(jnp.exp(math.log(0.1) - 6.7083283 * jax.random.uniform(seeds[6], (H,), jnp.float32) ** steps_of(seeds[6], (H,), ((0, 16),), -0.2, 0.2)), 0.00012207031, 0.1),
        "expert_in": gaussian(seeds[7], (EXPERTS, D, FF), D ** -0.5, 0.125, ((0, 32), (2, 16))),
        "expert_out": gaussian(seeds[8], (EXPERTS, FF, D), FF ** -0.5, 0.09375, ((0, 32), (1, 16))),
    }


def block_scores(query_heads, key_block, slopes, first_valid, window):
    raw_scores = jnp.einsum("ihd,jhd->hij", query_heads.astype(jnp.float32), key_block.astype(jnp.float32)) * (HD ** -0.5)
    row_pos = lax.broadcasted_iota(jnp.int32, (query_heads.shape[0], key_block.shape[0]), 0)
    col_pos = lax.broadcasted_iota(jnp.int32, (query_heads.shape[0], key_block.shape[0]), 1)
    distance = row_pos - col_pos + window
    in_window = (distance >= 0) & (distance < window) & (col_pos >= first_valid)
    biased = raw_scores - slopes[:, None, None] * distance.astype(jnp.float32)[None]
    return jnp.where(in_window[None], biased, -jnp.inf)


def slot_positions(flat_ids):
    expert_cols = lax.broadcasted_iota(jnp.int32, flat_ids.shape + (EXPERTS,), 2)
    one_hot = (flat_ids[..., None] == expert_cols).astype(jnp.int32)
    before = jnp.cumsum(one_hot, axis=1) - one_hot
    return jnp.sum(before * one_hot, axis=2).astype(jnp.int32)


def reference(queries, key_rows, value_rows, out_grad, expert_ids, gate_values, alibi_slope, expert_in, expert_out):
    score_scale = HD ** -0.5
    window = WCH * BLOCK
    span = window + BLOCK
    zero_rows = jnp.zeros((window, D), jnp.bfloat16)
    keys_padded = jnp.concatenate([zero_rows, key_rows])
    values_padded = jnp.concatenate([zero_rows, value_rows])

    def block_inputs(block_id):
        start_row = (block_id * BLOCK).astype(jnp.int32)
        query_heads = lax.dynamic_slice_in_dim(queries, start_row, BLOCK, 0).reshape(BLOCK, H, HD)
        key_block = lax.dynamic_slice_in_dim(keys_padded, start_row, span, 0).reshape(span, H, HD)
        value_block = lax.dynamic_slice_in_dim(values_padded, start_row, span, 0).reshape(span, H, HD)
        first_valid = jnp.maximum(window - start_row, 0).astype(jnp.int32)
        return start_row, query_heads, key_block, value_block, first_valid

    def forward_block(block_id):
        start_row, query_heads, key_block, value_block, first_valid = block_inputs(block_id)
        scores = block_scores(query_heads, key_block, alibi_slope, first_valid, window)
        log_norm = jax.nn.logsumexp(scores, axis=2)
        weights = jnp.exp(scores - log_norm[:, :, None]).astype(jnp.bfloat16)
        attn = jnp.einsum("hij,jhd->ihd", weights.astype(jnp.float32), value_block.astype(jnp.float32))
        return attn.astype(jnp.bfloat16).reshape(BLOCK, D), log_norm

    block_ids = jnp.arange(N_SEQ, dtype=jnp.int32)
    attn_blocks, norms = lax.map(forward_block, block_ids)
    attn_out = attn_blocks.reshape(TOKENS, D)

    ids_blocks = expert_ids.reshape(N_SEQ, BLOCK, 2)
    flat_ids = jnp.concatenate([ids_blocks[:, :, 0], ids_blocks[:, :, 1]], axis=1)
    position = slot_positions(flat_ids)
    is_kept = position < CAP
    block_index = lax.broadcasted_iota(jnp.int32, flat_ids.shape, 0)
    grad_blocks = out_grad.reshape(N_SEQ, BLOCK, D)
    gate_blocks = gate_values.reshape(N_SEQ, BLOCK, 2)
    token_flat = jnp.concatenate([attn_blocks, attn_blocks], axis=1)
    grad_flat = jnp.concatenate([gate_blocks[:, :, 0:1] * grad_blocks.astype(jnp.float32), gate_blocks[:, :, 1:2] * grad_blocks.astype(jnp.float32)], axis=1).astype(jnp.bfloat16)
    tokens_in = jnp.zeros((EXPERTS, N_SEQ, CAP, D), jnp.bfloat16).at[flat_ids, block_index, position].set(token_flat, mode="drop")
    grad_in = jnp.zeros((EXPERTS, N_SEQ, CAP, D), jnp.bfloat16).at[flat_ids, block_index, position].set(grad_flat, mode="drop")
    slot_rows = N_SEQ * CAP
    group_width = FF // N_EXP

    def expert_backward(operands):
        tokens, grad_rows, weight_in, weight_out = operands
        tokens = tokens.reshape(slot_rows, D)
        grad_rows = grad_rows.reshape(slot_rows, D)
        pre_act = jnp.dot(tokens, weight_in, preferred_element_type=jnp.float32)
        logistic = jax.nn.sigmoid(pre_act)
        hidden = (pre_act * logistic).astype(jnp.bfloat16)
        through_out = jnp.dot(grad_rows, weight_out.T, preferred_element_type=jnp.float32)
        hidden_grad = (through_out * logistic * (1.0 + pre_act * (1.0 - logistic))).astype(jnp.bfloat16)
        out_weight_grad = jnp.dot(hidden.T, grad_rows, preferred_element_type=jnp.float32).astype(jnp.bfloat16)
        in_weight_grad = jnp.dot(tokens.T, hidden_grad, preferred_element_type=jnp.float32).astype(jnp.bfloat16)
        grouped_grad = hidden_grad.reshape(slot_rows, N_EXP, group_width).astype(jnp.float32)
        grouped_weight = weight_in.reshape(D, N_EXP, group_width).astype(jnp.float32)
        partial_sums = jnp.einsum("rbf,dbf->brd", grouped_grad, grouped_weight).astype(jnp.bfloat16)
        back = jnp.sum(partial_sums.astype(jnp.float32), axis=0).astype(jnp.bfloat16)
        return in_weight_grad, out_weight_grad, back.reshape(N_SEQ, CAP, D)

    expert_in_grad, expert_out_grad, back_all = lax.map(expert_backward, (tokens_in, grad_in, expert_in, expert_out))
    picked = back_all[flat_ids, block_index, jnp.minimum(position, CAP - 1)].astype(jnp.float32)
    picked = jnp.where(is_kept[:, :, None], picked, 0.0)
    attn_grad_blocks = (grad_blocks.astype(jnp.float32) + picked[:, :BLOCK] + picked[:, BLOCK:]).astype(jnp.bfloat16)
    attn_grad = attn_grad_blocks.reshape(TOKENS, D)

    def backward_block(block_id, carry):
        query_total, key_total, value_total = carry
        block_id = jnp.asarray(block_id).astype(jnp.int32)
        start_row, query_heads, key_block, value_block, first_valid = block_inputs(block_id)
        attn_heads = lax.dynamic_slice_in_dim(attn_out, start_row, BLOCK, 0).reshape(BLOCK, H, HD).astype(jnp.float32)
        grad_heads = lax.dynamic_slice_in_dim(attn_grad, start_row, BLOCK, 0).reshape(BLOCK, H, HD).astype(jnp.float32)
        log_norm = lax.dynamic_index_in_dim(norms, block_id, 0, keepdims=False)
        scores = block_scores(query_heads, key_block, alibi_slope, first_valid, window)
        probs_full = jnp.exp(scores - log_norm[:, :, None])
        weights = probs_full.astype(jnp.bfloat16)
        row_delta = jnp.einsum("ihd,ihd->hi", grad_heads, attn_heads)
        dprob = jnp.einsum("ihd,jhd->hij", grad_heads, value_block.astype(jnp.float32))
        dscore = (probs_full * (dprob - row_delta[:, :, None])).astype(jnp.bfloat16).astype(jnp.float32)
        query_part = (jnp.einsum("hij,jhd->ihd", dscore, key_block.astype(jnp.float32)) * score_scale).astype(jnp.bfloat16)
        key_part = (jnp.einsum("hij,ihd->jhd", dscore, query_heads.astype(jnp.float32)) * score_scale).reshape(span, D)
        value_part = jnp.einsum("hij,ihd->jhd", weights.astype(jnp.float32), grad_heads).reshape(span, D)
        query_total = lax.dynamic_update_slice_in_dim(query_total, query_part.reshape(BLOCK, D), start_row, 0)
        key_old = lax.dynamic_slice_in_dim(key_total, start_row, span, 0)
        key_total = lax.dynamic_update_slice_in_dim(key_total, key_old + key_part, start_row, 0)
        value_old = lax.dynamic_slice_in_dim(value_total, start_row, span, 0)
        value_total = lax.dynamic_update_slice_in_dim(value_total, value_old + value_part, start_row, 0)
        return query_total, key_total, value_total

    start_carry = (jnp.zeros((TOKENS, D), jnp.bfloat16), jnp.zeros((window + TOKENS, D), jnp.float32), jnp.zeros((window + TOKENS, D), jnp.float32))
    query_grad, key_total, value_total = lax.fori_loop(0, N_SEQ, backward_block, start_carry)
    key_grad = key_total[window:].astype(jnp.bfloat16)
    value_grad = value_total[window:].astype(jnp.bfloat16)
    return (query_grad, key_grad, value_grad, expert_in_grad, expert_out_grad)
```

```python
import functools

import jax
import jax.numpy as jnp
from jax import lax
from jax.experimental import pallas as pl
from jax.experimental.pallas import tpu as pltpu
from jax.sharding import PartitionSpec as P

HD = 128
WCH = 16
PAD = 32
F32 = jnp.float32
BF16 = jnp.bfloat16
MESH = pl.DeviceIdType.MESH
NEG = -1.0e30


def nt(a, b):
    return lax.dot_general(a, b, (((1,), (1,)), ((), ())), preferred_element_type=F32)


def nn(a, b):
    return lax.dot_general(a, b, (((1,), (0,)), ((), ())), preferred_element_type=F32)


def tn(a, b):
    return lax.dot_general(a, b, (((0,), (0,)), ((), ())), preferred_element_type=F32)


def transposed(a):
    return jnp.transpose(a.astype(F32)).astype(BF16)


def remote(src, dst, send_sem, recv_sem, device):
    return pltpu.make_async_remote_copy(
        src_ref=src,
        dst_ref=dst,
        send_sem=send_sem,
        recv_sem=recv_sem,
        device_id=device,
        device_id_type=MESH,
    )


class GatherRing:
    def __init__(self, count, me, device_of, view, sems, on_arrival=None):
        self.n, self.me, self.view, self.on_arrival = count, me, view, on_arrival
        self.half = count // 2
        self.right = device_of(lax.rem(me + 1, count))
        self.left = device_of(lax.rem(me + count - 1, count))
        self.sems = sems

    def block(self, direction, hops):
        return lax.rem(self.me + (self.n - hops if direction == 0 else hops), self.n)

    def sends(self, direction, k, part):
        return k < self.half - 1 or (k == self.half - 1 and part == direction)

    def copy(self, direction, k, part, hops):
        ref = self.view(self.block(direction, hops), part)
        i = 2 * k + part
        return remote(
            ref,
            ref,
            self.sems[2 * direction].at[i],
            self.sems[2 * direction + 1].at[i],
            self.right if direction == 0 else self.left,
        )

    def start(self):
        for part in range(2):
            for direction in range(2):
                if self.sends(direction, 0, part):
                    self.copy(direction, 0, part, 0).start()
        if self.on_arrival:
            for part in range(2):
                self.on_arrival(self.me, 0, part)

    def step(self, k, part):
        for direction in range(2):
            if not self.sends(direction, k - 1, part):
                continue
            self.copy(direction, k - 1, part, k).wait_recv()
            if self.sends(direction, k, part):
                self.copy(direction, k, part, k).start()
            if self.on_arrival:
                distance = (self.n - k if direction == 0 else k) % self.n
                self.on_arrival(self.block(direction, k), distance, part)

    def drain(self):
        for k in range(self.half):
            for part in range(2):
                for direction in range(2):
                    if self.sends(direction, k, part):
                        self.copy(direction, k, part, k).wait_send()


def scratch_table(E, Y, Z, BL, D, FL, CAP):
    R, RP, hz, hy = E * CAP, E * PAD, max(Z // 2, 1), max(Y // 2, 1)
    table = dict(
        k3=((3, BL, HD), BF16),
        v3=((3, BL, HD), BF16),
        kt3=((3, HD, BL), BF16),
        vt3=((3, HD, BL), BF16),
        qb=((Z, BL, HD), BF16),
        gb=((Z, BL, HD), BF16),
        cb=((BL, BL), F32),
        osend=((Z, HD, BL), BF16),
        orecv=((Z, HD, BL), BF16),
        lsend=((Z, 8, BL), F32),
        lrecv=((Z, 8, BL), F32),
        stats=((Z, 16, BL), F32),
        ot=((HD, BL), BF16),
        ogt=((HD, BL), F32),
        routing=((RP, 2 * BL), BF16),
        comp=((R, RP), BF16),
        compt=((RP, R), BF16),
        gs=((E, PAD, HD), BF16),
        gr=((E, PAD, HD), BF16),
        ts=((E, PAD, HD), BF16),
        tr=((E, PAD, HD), BF16),
        bs=((E, PAD, HD), BF16),
        br=((E, PAD, HD), BF16),
        grads=((2 * Y, R, HD), BF16),
        toks=((2 * Y, R, HD), BF16),
        win=((D, FL), BF16),
        wout=((FL, D), BF16),
        thr=((R, FL), F32),
        pre=((R, FL), F32),
        hid=((FL, R), BF16),
        hg=((R, FL), BF16),
        pb=((Y, R, HD), BF16),
        sb=((Y, R, HD), BF16),
        rb=((Y, R, HD), BF16),
        rs_stage=((2, 2 * hy, R // 2, HD), BF16),
        rs_recv=((2, 2 * hy, R // 2, HD), BF16),
        dwi=((D, FL), BF16),
        dwo=((FL, D), BF16),
        dk3=((3, BL, HD), F32),
        dv3=((3, BL, HD), F32),
        dksend=((2, BL, HD), BF16),
        dvsend=((2, BL, HD), BF16),
        dkrecv=((2, BL, HD), BF16),
        dvrecv=((2, BL, HD), BF16),
        dqsend=((Z, HD, BL), BF16),
        dqrecv=((Z, HD, BL), BF16),
        dqown=((HD, BL), F32),
    )
    shapes = {name: pltpu.VMEM(shape, dtype) for name, (shape, dtype) in table.items()}
    counts = dict(
        kv_s=4, kv_r=4, o_s=Z, o_r=Z, l_s=Z, l_r=Z, st_s=Z, st_r=Z, dq_s=Z, dq_r=Z, dkv_s=4, dkv_r=4,
        ga_s=E, ga_r=E, ta_s=E, ta_r=E, ba_s=E, ba_r=E, w=2, dw=2,
        gsib_s=2 * Y, gsib_r=2 * Y, tsib_s=2 * Y, tsib_r=2 * Y, psib_s=Y, psib_r=Y,
    )
    for ring, half in (("q", hz), ("g", hz), ("ygr", hy), ("ytk", hy), ("rs", hy)):
        for end in ("_rs", "_rr", "_ls", "_lr"):
            counts[ring + end] = 2 * half
    for name, count in counts.items():
        shapes["sem_" + name] = pltpu.SemaphoreType.DMA((count,))
    return shapes


def body(names, E, Y, Z, CAP, *refs):
    (q_ref, k_ref, v_ref, og_ref, ids_ref, gates_ref, slope_ref, win_ref, wout_ref,
     dq_ref, dk_ref, dv_ref, dwi_ref, dwo_ref) = refs[:14]
    S = dict(zip(names, refs[14:]))
    BL, FL = q_ref.shape[0], win_ref.shape[2]
    X, R, RP, D = E // Z, E * CAP, E * PAD, 2 * Y * HD
    scale = HD ** (-0.5)
    s, e = lax.axis_index("seq"), lax.axis_index("exp")
    x, z = lax.div(s, Z), lax.rem(s, Z)
    y, c = lax.div(e, 2), lax.rem(e, 2)
    sibling = (s, 2 * y + 1 - c)

    def zdev(j):
        return (x * Z + j, e)

    def xdev(i):
        return (lax.rem(i, X) * Z + z, e)

    def ydev(j):
        return (s, 2 * j + c)

    weights_in = [
        pltpu.make_async_copy(win_ref.at[0], S["win"], S["sem_w"].at[0]),
        pltpu.make_async_copy(wout_ref.at[0], S["wout"], S["sem_w"].at[1]),
    ]
    for copy in weights_in:
        copy.start()

    barrier = pltpu.get_barrier_semaphore()

    def greet(i, carry):
        pl.semaphore_signal(
            barrier, inc=1, device_id=(lax.rem(s + i, E), e), device_id_type=MESH
        )
        return carry

    lax.fori_loop(1, E, greet, 0)
    for device in (ydev(lax.rem(y + 1, Y)), ydev(lax.rem(y + Y - 1, Y)), sibling):
        pl.semaphore_signal(barrier, inc=1, device_id=device, device_id_type=MESH)

    S["qb"][z] = q_ref[...]
    S["k3"][0] = k_ref[...]
    S["v3"][0] = v_ref[...]
    S["kt3"][0] = transposed(k_ref[...])
    S["vt3"][0] = transposed(v_ref[...])
    pl.semaphore_wait(barrier, E - 1 + 3)

    q_ring = GatherRing(
        Z, z, zdev, lambda b, p: S["qb"].at[b, pl.ds(p * (BL // 2), BL // 2), :],
        [S["sem_q_rs"], S["sem_q_rr"], S["sem_q_ls"], S["sem_q_lr"]],
    )
    q_ring.start()
    kv_copies = []
    for hop in (1, 2):
        for which, (own, buf) in enumerate((("k3", "k3"), ("v3", "v3"))):
            i = 2 * (hop - 1) + which
            copy = remote(
                S[own].at[0], S[buf].at[hop], S["sem_kv_s"].at[i], S["sem_kv_r"].at[i],
                xdev(x + hop),
            )
            copy.start()
            kv_copies.append(copy)

    flat = jnp.concatenate([ids_ref[0:1, :], ids_ref[1:2, :]], axis=1)
    hot = lax.broadcasted_iota(jnp.int32, (E, 2 * BL), 0) == flat
    hot_f = jnp.where(hot, 1.0, 0.0)
    upper = lax.broadcasted_iota(jnp.int32, (2 * BL, 2 * BL), 0) < lax.broadcasted_iota(
        jnp.int32, (2 * BL, 2 * BL), 1
    )
    before = nn(hot_f.astype(BF16), jnp.where(upper, 1.0, 0.0).astype(BF16))
    position = jnp.sum(before * hot_f, axis=0, keepdims=True)
    slot = jnp.where(position < CAP, flat * PAD + position.astype(jnp.int32), -1)
    S["routing"][...] = jnp.where(
        lax.broadcasted_iota(jnp.int32, (RP, 2 * BL), 0) == slot, 1.0, 0.0
    ).astype(BF16)
    ogt = jnp.transpose(og_ref[...].astype(F32))
    S["ogt"][...] = ogt
    scaled = jnp.concatenate([ogt * gates_ref[0:1, :], ogt * gates_ref[1:2, :]], axis=1)
    S["gs"][...] = nt(S["routing"][...], scaled.astype(BF16)).astype(BF16).reshape(E, PAD, HD)

    def exchange_start(send, recv, send_sem, recv_sem):
        recv[s] = send[s]

        def go(i, carry):
            peer = lax.rem(s + i, E)
            remote(send.at[peer], recv.at[s], send_sem.at[i], recv_sem.at[i], (peer, e)).start()
            return carry

        lax.fori_loop(1, E, go, 0)

    def exchange_wait(send, recv, send_sem, recv_sem):
        def go(i, carry):
            peer = lax.rem(s + E - i, E)
            remote(send.at[peer], recv.at[peer], send_sem.at[i], recv_sem.at[i], (peer, e)).wait_recv()
            return carry

        lax.fori_loop(1, E, go, 0)

    def exchange_drain(send, recv, send_sem, recv_sem):
        def go(i, carry):
            peer = lax.rem(s + i, E)
            remote(send.at[peer], recv.at[s], send_sem.at[i], recv_sem.at[i], (peer, e)).wait_send()
            return carry

        lax.fori_loop(1, E, go, 0)

    grad_exchange = (S["gs"], S["gr"], S["sem_ga_s"], S["sem_ga_r"])
    token_exchange = (S["ts"], S["tr"], S["sem_ta_s"], S["sem_ta_r"])
    back_exchange = (S["bs"], S["br"], S["sem_ba_s"], S["sem_ba_r"])
    exchange_start(*grad_exchange)

    padded = lax.broadcasted_iota(jnp.int32, (1, RP), 1)
    packed_of = jnp.where(
        (padded & (PAD - 1)) < CAP, (padded >> 5) * CAP + (padded & (PAD - 1)), -1
    )
    S["comp"][...] = jnp.where(
        lax.broadcasted_iota(jnp.int32, (R, RP), 0) == packed_of, 1.0, 0.0
    ).astype(BF16)

    slope = slope_ref[0]
    S["cb"][...] = lax.broadcasted_iota(jnp.int32, (BL, BL), 0).astype(F32) * slope
    causal = lax.broadcasted_iota(jnp.int32, (BL, BL), 0) <= lax.broadcasted_iota(
        jnp.int32, (BL, BL), 1
    )

    def pieces(d, j):
        def offset(r):
            distance = ((j - z) * BL).astype(F32) + float(r * Z * BL)
            return jnp.where(x >= r, 0.0, NEG) - slope * distance

        if d == 0:
            return [(0, offset(0), causal), (1, offset(1), None), (2, offset(2), ~causal)]
        r = jnp.where(j > z, 0, 2)
        near = jnp.where(j > z, offset(0), offset(2))
        return [(r, near, None), (1, offset(1), None)]

    def scores_of(r, offset, mask, queries):
        raw = nt(S["k3"][r], queries) * scale + (S["cb"][...] + offset)
        return raw if mask is None else jnp.where(mask, raw, NEG)

    def forward(d):
        j = lax.rem(z + d, Z)
        queries = S["qb"][j]
        parts = pieces(d, j)
        scores = [scores_of(r, offset, mask, queries) for r, offset, mask in parts]
        top = functools.reduce(
            jnp.maximum, [jnp.max(t, axis=0, keepdims=True) for t in scores]
        )
        total, out = 0.0, 0.0
        for (r, _, _), t in zip(parts, scores):
            p = jnp.exp(t - top)
            total = total + jnp.sum(p, axis=0, keepdims=True)
            out = out + nn(S["vt3"][r], p.astype(BF16))
        out = (out / total).astype(BF16)
        log_norm = jnp.broadcast_to(top + jnp.log(total), (8, BL))
        if d == 0:
            S["orecv"][0] = out
            S["lrecv"][0] = log_norm
            return
        S["osend"][d] = out
        S["lsend"][d] = log_norm
        out_copy(d).start()
        norm_copy(d).start()

    def out_copy(d):
        return remote(S["osend"].at[d], S["orecv"].at[d], S["sem_o_s"].at[d], S["sem_o_r"].at[d],
                      zdev(lax.rem(z + d, Z)))

    def norm_copy(d):
        return remote(S["lsend"].at[d], S["lrecv"].at[d], S["sem_l_s"].at[d], S["sem_l_r"].at[d],
                      zdev(lax.rem(z + d, Z)))

    for copy in kv_copies:
        copy.wait_recv()
    for r in (1, 2):
        S["kt3"][r] = transposed(S["k3"][r])
        S["vt3"][r] = transposed(S["v3"][r])
    forward(0)

    def feature_ring(buf, ring, sib):
        def arrived(block, distance, part):
            sib_copy(buf, sib, block, distance, part).start()

        return GatherRing(
            Y, y, ydev, lambda b, p: buf.at[2 * b + c, pl.ds(p * (R // 2), R // 2), :],
            [S["sem_" + ring + end] for end in ("_rs", "_rr", "_ls", "_lr")], arrived,
        )

    def sib_copy(buf, sib, block, distance, part):
        ref = buf.at[2 * block + c, pl.ds(part * (R // 2), R // 2), :]
        i = 2 * distance + part
        return remote(ref, ref, S["sem_" + sib + "_s"].at[i], S["sem_" + sib + "_r"].at[i], sibling)

    def sib_wait(buf, sib, distance):
        block = lax.rem(y + distance, Y)
        for part in range(2):
            ref = buf.at[2 * block + 1 - c, pl.ds(part * (R // 2), R // 2), :]
            i = 2 * distance + part
            remote(ref, ref, S["sem_" + sib + "_s"].at[i], S["sem_" + sib + "_r"].at[i], sibling).wait_recv()

    def sib_drain(buf, sib):
        for distance in range(Y):
            for part in range(2):
                sib_copy(buf, sib, lax.rem(y + distance, Y), distance, part).wait_send()

    exchange_wait(*grad_exchange)
    S["grads"][e] = nn(S["comp"][...], S["gr"][...].reshape(RP, HD)).astype(BF16)
    grad_ring = feature_ring(S["grads"], "ygr", "gsib")
    grad_ring.start()
    grad_steps = [(k, p) for k in range(1, Y // 2 + 1) for p in range(2)]

    def advance_grads():
        if grad_steps:
            grad_ring.step(*grad_steps.pop(0))

    for k in range(1, Z // 2 + 1):
        for part in range(2):
            q_ring.step(k, part)
        for d in sorted({k, Z - k}):
            forward(d)
        advance_grads()

    for d in range(1, Z):
        out_copy(d).wait_recv()
        norm_copy(d).wait_recv()
    norms = [S["lrecv"][d][0:1, :] for d in range(Z)]
    top = functools.reduce(jnp.maximum, norms)
    shares = [jnp.exp(t - top) for t in norms]
    total = functools.reduce(jnp.add, shares)
    merged = functools.reduce(
        jnp.add, [S["orecv"][d].astype(F32) * shares[d] for d in range(Z)]
    )
    out_t = (merged / total).astype(BF16)
    S["ot"][...] = out_t
    log_norm = top + jnp.log(total)
    S["stats"][z, 0:8, :] = jnp.broadcast_to(log_norm, (8, BL))

    S["ts"][...] = (
        nt(S["routing"][...], jnp.concatenate([out_t, out_t], axis=1))
        .astype(BF16)
        .reshape(E, PAD, HD)
    )
    exchange_start(*token_exchange)

    def pair(buf, block):
        return jnp.concatenate([buf[2 * block], buf[2 * block + 1]], axis=1)

    def columns(block):
        return pl.ds(pl.multiple_of(block * (2 * HD), 2 * HD), 2 * HD)

    order = [0]
    for k in range(1, Y // 2 + 1):
        order += sorted({k, Y - k})

    for copy in weights_in:
        copy.wait()
    while grad_steps:
        advance_grads()
    for n, d in enumerate(order):
        sib_wait(S["grads"], "gsib", d)
        block = lax.rem(y + d, Y)
        term = nt(pair(S["grads"], block), S["wout"][:, columns(block)])
        S["thr"][...] = term if n == 0 else S["thr"][...] + term

    exchange_wait(*token_exchange)
    S["toks"][e] = nn(S["comp"][...], S["tr"][...].reshape(RP, HD)).astype(BF16)
    token_ring = feature_ring(S["toks"], "ytk", "tsib")
    token_ring.start()
    slots = lax.broadcasted_iota(jnp.int32, (RP, R), 0)
    packed_rows = jnp.where(
        (slots & (PAD - 1)) < CAP, (slots >> 5) * CAP + (slots & (PAD - 1)), -1
    )
    S["compt"][...] = jnp.where(
        packed_rows == lax.broadcasted_iota(jnp.int32, (RP, R), 1), 1.0, 0.0
    ).astype(BF16)

    def pre_term(d):
        sib_wait(S["toks"], "tsib", d)
        block = lax.rem(y + d, Y)
        term = nn(pair(S["toks"], block), S["win"][columns(block), :])
        S["pre"][...] = term if d == 0 else S["pre"][...] + term

    pre_term(0)
    for k in range(1, Y // 2 + 1):
        for part in range(2):
            token_ring.step(k, part)
        for d in sorted({k, Y - k}):
            pre_term(d)

    pre = S["pre"][...]
    logistic = 1.0 / (1.0 + jnp.exp(-pre))
    S["hid"][...] = jnp.transpose(pre * logistic).astype(BF16)
    S["hg"][...] = (S["thr"][...] * logistic * (1.0 + pre * (1.0 - logistic))).astype(BF16)

    def partner_copy(distance):
        block = lax.rem(y + distance, Y)
        return remote(S["sb"].at[block], S["rb"].at[block], S["sem_psib_s"].at[distance],
                      S["sem_psib_r"].at[distance], sibling)

    far_first = order[::-1]
    for d in far_first:
        block = lax.rem(y + d, Y)
        share = nt(S["hg"][...], S["win"][columns(block), :]).astype(BF16)
        first, second = share[:, :HD], share[:, HD:]
        S["pb"][block] = jnp.where(c == 0, first, second)
        S["sb"][block] = jnp.where(c == 0, second, first)
        partner_copy(d).start()

    half = Y // 2
    rows = R // 2

    def hops(direction, chunk):
        return half if direction == chunk else half - 1

    def ring_copy(direction, chunk, h):
        i = 2 * h + chunk
        ends = ("_rs", "_rr") if direction == 0 else ("_ls", "_lr")
        neighbour = ydev(lax.rem(y + 1, Y)) if direction == 0 else ydev(lax.rem(y + Y - 1, Y))
        return remote(S["rs_stage"].at[direction, i], S["rs_recv"].at[direction, i],
                      S["sem_rs" + ends[0]].at[i], S["sem_rs" + ends[1]].at[i], neighbour)

    def own_part(block, chunk):
        span = pl.ds(chunk * rows, rows)
        return S["pb"][block, span, :].astype(F32) + S["rb"][block, span, :].astype(F32)

    weight_work = [("out", d) for d in order] + [("in", d) for d in order]

    def some_weight_work(count):
        for _ in range(min(count, len(weight_work))):
            which, d = weight_work.pop(0)
            block = lax.rem(y + d, Y)
            if which == "out":
                S["dwo"][:, columns(block)] = nn(S["hid"][...], pair(S["grads"], block)).astype(BF16)
            else:
                S["dwi"][columns(block), :] = tn(pair(S["toks"], block), S["hg"][...]).astype(BF16)

    waited = set()

    def need_partner(distance):
        if distance not in waited:
            waited.add(distance)
            partner_copy(distance).wait_recv()

    per_hop = -(-2 * Y // half)
    for h in range(half):
        for direction, chunk in ((0, 0), (1, 1), (0, 1), (1, 0)):
            total_hops = hops(direction, chunk)
            if h >= total_hops:
                continue
            distance = total_hops - h if direction == 0 else Y - (total_hops - h)
            need_partner(distance)
            value = own_part(lax.rem(y + distance, Y), chunk)
            if h > 0:
                ring_copy(direction, chunk, h - 1).wait_recv()
                value = value + S["rs_recv"][direction, 2 * (h - 1) + chunk].astype(F32)
            S["rs_stage"][direction, 2 * h + chunk] = value.astype(BF16)
            ring_copy(direction, chunk, h).start()
        some_weight_work(per_hop)
    need_partner(0)
    sums = []
    for chunk in range(2):
        value = own_part(y, chunk)
        for direction in range(2):
            last = hops(direction, chunk) - 1
            if last >= 0:
                ring_copy(direction, chunk, last).wait_recv()
                value = value + S["rs_recv"][direction, 2 * last + chunk].astype(F32)
        sums.append(value.astype(BF16))
    back = jnp.concatenate(sums, axis=0)
    S["bs"][...] = nn(S["compt"][...], back).astype(BF16).reshape(E, PAD, HD)
    exchange_start(*back_exchange)
    some_weight_work(2 * Y)
    weights_out = [
        pltpu.make_async_copy(S["dwi"], dwi_ref.at[0], S["sem_dw"].at[0]),
        pltpu.make_async_copy(S["dwo"], dwo_ref.at[0], S["sem_dw"].at[1]),
    ]
    for copy in weights_out:
        copy.start()
    exchange_wait(*back_exchange)
    combined = tn(S["br"][...].reshape(RP, HD), S["routing"][...])
    grad_t = (S["ogt"][...] + combined[:, :BL] + combined[:, BL:]).astype(BF16).astype(F32)
    delta = jnp.sum(grad_t * S["ot"][...].astype(F32), axis=0, keepdims=True)
    S["stats"][z, 8:16, :] = jnp.broadcast_to(delta, (8, BL))
    S["gb"][z] = jnp.transpose(grad_t).astype(BF16)

    g_ring = GatherRing(
        Z, z, zdev, lambda b, p: S["gb"].at[b, pl.ds(p * (BL // 2), BL // 2), :],
        [S["sem_g_rs"], S["sem_g_rr"], S["sem_g_ls"], S["sem_g_lr"]],
    )

    def stats_copy(d, block):
        ref = S["stats"].at[block]
        return remote(ref, ref, S["sem_st_s"].at[d], S["sem_st_r"].at[d], zdev(lax.rem(z + d, Z)))

    for d in range(1, Z):
        stats_copy(d, z).start()
    g_ring.start()

    def dq_copy(d):
        return remote(S["dqsend"].at[d], S["dqrecv"].at[d], S["sem_dq_s"].at[d], S["sem_dq_r"].at[d],
                      zdev(lax.rem(z + d, Z)))

    def backward(d):
        j = lax.rem(z + d, Z)
        queries, grads = S["qb"][j], S["gb"][j]
        norm, dlt = S["stats"][j, 0:1, :], S["stats"][j, 8:9, :]
        dq = 0.0
        for r, offset, mask in pieces(d, j):
            p = jnp.exp(scores_of(r, offset, mask, queries) - norm)
            dv = nn(p.astype(BF16), grads)
            ds = (p * (nt(S["v3"][r], grads) - dlt)).astype(BF16)
            dk = nn(ds, queries)
            dq = dq + nn(S["kt3"][r], ds)
            if d == 0:
                S["dv3"][r], S["dk3"][r] = dv, dk
            else:
                S["dv3"][r] = S["dv3"][r] + dv
                S["dk3"][r] = S["dk3"][r] + dk
        dq = dq * scale
        if d == 0:
            S["dqown"][...] = dq
        else:
            S["dqsend"][d] = dq.astype(BF16)
            dq_copy(d).start()

    backward(0)
    for k in range(1, Z // 2 + 1):
        for part in range(2):
            g_ring.step(k, part)
        for d in sorted({k, Z - k}):
            stats_copy(Z - d, lax.rem(z + d, Z)).wait_recv()
            backward(d)

    dkv_copies = []
    for hop in (1, 2):
        S["dksend"][hop - 1] = (S["dk3"][hop] * scale).astype(BF16)
        S["dvsend"][hop - 1] = S["dv3"][hop].astype(BF16)
        for which, name in enumerate(("dk", "dv")):
            i = 2 * (hop - 1) + which
            copy = remote(S[name + "send"].at[hop - 1], S[name + "recv"].at[hop - 1],
                          S["sem_dkv_s"].at[i], S["sem_dkv_r"].at[i], xdev(x + X - hop))
            copy.start()
            dkv_copies.append(copy)

    dq = S["dqown"][...]
    for d in range(1, Z):
        dq_copy(d).wait_recv()
        dq = dq + S["dqrecv"][d].astype(F32)
    dq_ref[...] = jnp.transpose(dq).astype(BF16)
    for copy in dkv_copies:
        copy.wait_recv()
    dk_ref[...] = (
        S["dk3"][0] * scale + S["dkrecv"][0].astype(F32) + S["dkrecv"][1].astype(F32)
    ).astype(BF16)
    dv_ref[...] = (
        S["dv3"][0] + S["dvrecv"][0].astype(F32) + S["dvrecv"][1].astype(F32)
    ).astype(BF16)

    for copy in kv_copies + dkv_copies:
        copy.wait_send()
    for ring in (q_ring, g_ring, grad_ring, token_ring):
        ring.drain()
    for d in range(1, Z):
        out_copy(d).wait_send()
        norm_copy(d).wait_send()
        stats_copy(d, z).wait_send()
        dq_copy(d).wait_send()
    for exchange in (grad_exchange, token_exchange, back_exchange):
        exchange_drain(*exchange)
    sib_drain(S["grads"], "gsib")
    sib_drain(S["toks"], "tsib")
    for d in range(Y):
        partner_copy(d).wait_send()
    for direction in range(2):
        for chunk in range(2):
            for h in range(hops(direction, chunk)):
                ring_copy(direction, chunk, h).wait_send()
    for copy in weights_out:
        copy.wait()


def per_device(
    queries,
    key_rows,
    value_rows,
    out_grad,
    expert_ids,
    gate_values,
    alibi_slope,
    expert_in,
    expert_out,
):
    E, N = lax.axis_size("seq"), lax.axis_size("exp")
    Y, Z = N // 2, WCH // 2
    BL = queries.shape[0]
    D, FL = expert_in.shape[1:]
    CAP = 5 * BL // (2 * E)
    scratch = scratch_table(E, Y, Z, BL, D, FL, CAP)
    vmem = pl.BlockSpec(memory_space=pltpu.VMEM)
    smem = pl.BlockSpec(memory_space=pltpu.SMEM)
    hbm = pl.BlockSpec(memory_space=pl.ANY)
    shape = jax.ShapeDtypeStruct
    return pl.pallas_call(
        functools.partial(body, list(scratch), E, Y, Z, CAP),
        out_shape=(
            shape(queries.shape, BF16),
            shape(queries.shape, BF16),
            shape(queries.shape, BF16),
            shape(expert_in.shape, BF16),
            shape(expert_out.shape, BF16),
        ),
        in_specs=[vmem] * 6 + [smem] + [hbm] * 2,
        out_specs=(vmem, vmem, vmem, hbm, hbm),
        scratch_shapes=list(scratch.values()),
        compiler_params=pltpu.CompilerParams(
            collective_id=0, has_side_effects=True, vmem_limit_bytes=56 * 2**20
        ),
    )(
        queries,
        key_rows,
        value_rows,
        out_grad,
        expert_ids.T,
        gate_values.T,
        alibi_slope,
        expert_in,
        expert_out,
    )


def solution(mesh):
    return jax.shard_map(
        per_device,
        mesh=mesh,
        in_specs=(
            P("seq", "exp"),
            P("seq", "exp"),
            P("seq", "exp"),
            P("seq", "exp"),
            P("seq", None),
            P("seq", None),
            P("exp"),
            P("seq", None, "exp"),
            P("seq", "exp", None),
        ),
        out_specs=(
            P("seq", "exp"),
            P("seq", "exp"),
            P("seq", "exp"),
            P("seq", None, "exp"),
            P("seq", "exp", None),
        ),
        check_vma=False,
    )
```

```python
import functools

import jax
import jax.numpy as jnp
from jax import lax
from jax.experimental import pallas as pl
from jax.experimental.pallas import tpu as pltpu
from jax.sharding import PartitionSpec as P

HD = 128
WCH = 16
PAD = 24
F32 = jnp.float32
BF16 = jnp.bfloat16
MESH = pl.DeviceIdType.MESH
NEG = -1.0e30


def nt(a, b):
    return lax.dot_general(a, b, (((1,), (1,)), ((), ())), preferred_element_type=F32)


def nn(a, b):
    return lax.dot_general(a, b, (((1,), (0,)), ((), ())), preferred_element_type=F32)


def tn(a, b):
    return lax.dot_general(a, b, (((0,), (0,)), ((), ())), preferred_element_type=F32)


def transposed(a):
    return jnp.transpose(a.astype(F32)).astype(BF16)


def remote(src, dst, send_sem, recv_sem, device):
    return pltpu.make_async_remote_copy(
        src_ref=src,
        dst_ref=dst,
        send_sem=send_sem,
        recv_sem=recv_sem,
        device_id=device,
        device_id_type=MESH,
    )


class GatherRing:
    def __init__(self, count, parts, me, device_of, view, sems, on_arrival=None):
        self.n, self.parts, self.me, self.view, self.on_arrival = count, parts, me, view, on_arrival
        self.half = count // 2
        self.right = device_of(lax.rem(me + 1, count))
        self.left = device_of(lax.rem(me + count - 1, count))
        self.sems = sems

    def block(self, direction, hops):
        return lax.rem(self.me + (self.n - hops if direction == 0 else hops), self.n)

    def sends(self, direction, k, part):
        return k < self.half - 1 or (k == self.half - 1 and self.ahead(direction, part))

    def ahead(self, direction, part):
        return (part < self.parts // 2) == (direction == 0)

    def copy(self, direction, k, part, hops):
        ref = self.view(self.block(direction, hops), part)
        i = self.parts * k + part
        return remote(
            ref,
            ref,
            self.sems[2 * direction].at[i],
            self.sems[2 * direction + 1].at[i],
            self.right if direction == 0 else self.left,
        )

    def start(self, part):
        for direction in range(2):
            if self.sends(direction, 0, part):
                self.copy(direction, 0, part, 0).start()
        if self.on_arrival:
            self.on_arrival(self.me, 0, part)

    def step(self, k, part):
        for direction in range(2):
            if not self.sends(direction, k - 1, part):
                continue
            self.copy(direction, k - 1, part, k).wait_recv()
            if self.sends(direction, k, part):
                self.copy(direction, k, part, k).start()
            if self.on_arrival:
                distance = (self.n - k if direction == 0 else k) % self.n
                self.on_arrival(self.block(direction, k), distance, part)

    def drain(self):
        for k in range(self.half):
            for part in range(self.parts):
                for direction in range(2):
                    if self.sends(direction, k, part):
                        self.copy(direction, k, part, k).wait_send()


def scratch_table(E, Y, Z, BL, D, FL, CAP):
    R, RP, hz, hy, X = E * CAP, E * PAD, max(Z // 2, 1), max(Y // 2, 1), E // Z
    table = dict(
        k3=((3, BL, HD), BF16),
        v3=((3, BL, HD), BF16),
        kt3=((3, HD, BL), BF16),
        vt3=((3, HD, BL), BF16),
        qb=((Z, BL, HD), BF16),
        gb=((Z, BL, HD), BF16),
        cb=((BL, BL), F32),
        osend=((Z, HD, BL), BF16),
        orecv=((Z, HD, BL), BF16),
        lsend=((Z, 1, BL), F32),
        lrecv=((Z, 1, BL), F32),
        stats=((Z, 2, BL), F32),
        ot=((HD, BL), BF16),
        ogt=((HD, BL), F32),
        routing=((RP, 2 * BL), BF16),
        comp=((R // X, RP // X), BF16),
        compt=((RP // X, R // X), BF16),
        gs=((E, PAD, HD), BF16),
        gr=((E, PAD, HD), BF16),
        ts=((E, PAD, HD), BF16),
        tr=((E, PAD, HD), BF16),
        bs=((E, PAD, HD), BF16),
        br=((E, PAD, HD), BF16),
        grads=((2 * Y, R, HD), BF16),
        toks=((2 * Y, R, HD), BF16),
        win=((D, FL), BF16),
        wout=((FL, D), BF16),
        thr=((R, FL), F32),
        pre=((R, FL), F32),
        hid=((FL, R), BF16),
        hg=((R, FL), BF16),
        pb=((Y, R, HD), BF16),
        sb=((Y, R, HD), BF16),
        rb=((Y, R, HD), BF16),
        rs_stage=((2, X * hy, R // X, HD), BF16),
        rs_recv=((2, X * hy, R // X, HD), BF16),
        dwi=((D, FL), BF16),
        dwo=((FL, D), BF16),
        dk3=((3, BL, HD), F32),
        dv3=((3, BL, HD), F32),
        dksend=((2, BL, HD), BF16),
        dvsend=((2, BL, HD), BF16),
        dkrecv=((2, BL, HD), BF16),
        dvrecv=((2, BL, HD), BF16),
        dqsend=((Z, HD, BL), BF16),
        dqrecv=((Z, HD, BL), BF16),
        dqown=((HD, BL), F32),
    )
    shapes = {name: pltpu.VMEM(shape, dtype) for name, (shape, dtype) in table.items()}
    counts = dict(
        kv_s=4, kv_r=4, o_s=Z, o_r=Z, l_s=Z, l_r=Z, st_s=Z, st_r=Z, dq_s=Z, dq_r=Z, dkv_s=4, dkv_r=4,
        ga_s=E, ga_r=E, ta_s=E, ta_r=E, ba_s=E, ba_r=E, w=2, dw=2,
        gsib_s=X * Y, gsib_r=X * Y, tsib_s=X * Y, tsib_r=X * Y, psib_s=Y, psib_r=Y,
    )
    for ring, half in (("q", 2 * hz), ("g", 2 * hz), ("ygr", X * hy), ("ytk", X * hy), ("rs", X * hy)):
        for end in ("_rs", "_rr", "_ls", "_lr"):
            counts[ring + end] = half
    for name, count in counts.items():
        shapes["sem_" + name] = pltpu.SemaphoreType.DMA((count,))
    shapes["columns_in"] = pltpu.SemaphoreType.REGULAR
    return shapes


def body(names, E, Y, Z, CAP, *refs):
    (q_ref, k_ref, v_ref, og_ref, ids_ref, gates_ref, slope_ref, win_ref, wout_ref,
     dq_ref, dk_ref, dv_ref, dwi_ref, dwo_ref) = refs[:14]
    S = dict(zip(names, refs[14:]))
    BL, FL = q_ref.shape[0], win_ref.shape[2]
    X, R, RP, D = E // Z, E * CAP, E * PAD, 2 * Y * HD
    scale = HD ** (-0.5)
    s, e = lax.axis_index("seq"), lax.axis_index("exp")
    x, z = lax.div(s, Z), lax.rem(s, Z)
    y, c = lax.div(e, 2), lax.rem(e, 2)
    sibling = (s, 2 * y + 1 - c)

    def zdev(j):
        return (x * Z + j, e)

    def xdev(i):
        return (lax.rem(i, X) * Z + z, e)

    def ydev(j):
        return (s, 2 * j + c)

    drains = []
    barrier = pltpu.get_barrier_semaphore()
    near = [zdev(lax.rem(z + d, Z)) for d in range(1, Z)] + [xdev(x + d) for d in range(1, X)]
    near += [ydev(lax.rem(y + 1, Y)), ydev(lax.rem(y + Y - 1, Y)), sibling]
    for device in near:
        pl.semaphore_signal(barrier, inc=1, device_id=device, device_id_type=MESH)

    weights_in = [
        pltpu.make_async_copy(win_ref.at[0], S["win"], S["sem_w"].at[0]),
        pltpu.make_async_copy(wout_ref.at[0], S["wout"], S["sem_w"].at[1]),
    ]
    for copy in weights_in:
        copy.start()
    S["qb"][z] = q_ref[...]
    S["k3"][0] = k_ref[...]
    S["v3"][0] = v_ref[...]
    pl.semaphore_wait(barrier, len(near))

    q_ring = GatherRing(
        Z, 2, z, zdev, lambda b, p: S["qb"].at[b, pl.ds(p * (BL // 2), BL // 2), :],
        [S["sem_q_rs"], S["sem_q_rr"], S["sem_q_ls"], S["sem_q_lr"]],
    )
    for part in range(2):
        q_ring.start(part)
    drains.append(q_ring.drain)
    kv_copies = []
    for hop in (1, 2):
        for which, (own, buf) in enumerate((("k3", "k3"), ("v3", "v3"))):
            i = 2 * (hop - 1) + which
            copy = remote(
                S[own].at[0], S[buf].at[hop], S["sem_kv_s"].at[i], S["sem_kv_r"].at[i],
                xdev(x + hop),
            )
            copy.start()
            kv_copies.append(copy)
            drains.append(copy.wait_send)

    for d in range(1, X):
        pl.semaphore_signal(
            S["columns_in"], inc=1, device_id=xdev(x + d), device_id_type=MESH
        )

    flat = jnp.concatenate([ids_ref[0:1, :], ids_ref[1:2, :]], axis=1)
    hot = lax.broadcasted_iota(jnp.int32, (E, 2 * BL), 0) == flat
    hot_f = jnp.where(hot, 1.0, 0.0)
    upper = lax.broadcasted_iota(jnp.int32, (2 * BL, 2 * BL), 0) < lax.broadcasted_iota(
        jnp.int32, (2 * BL, 2 * BL), 1
    )
    before = nn(hot_f.astype(BF16), jnp.where(upper, 1.0, 0.0).astype(BF16))
    position = jnp.sum(before * hot_f, axis=0, keepdims=True)
    slot = jnp.where(position < CAP, flat * PAD + position.astype(jnp.int32), -1)
    S["routing"][...] = jnp.where(
        lax.broadcasted_iota(jnp.int32, (RP, 2 * BL), 0) == slot, 1.0, 0.0
    ).astype(BF16)
    ogt = jnp.transpose(og_ref[...].astype(F32))
    S["ogt"][...] = ogt
    scaled = jnp.concatenate([ogt * gates_ref[0:1, :], ogt * gates_ref[1:2, :]], axis=1)
    def spread(send, value):
        send[...] = value.reshape(E, PAD, HD).astype(BF16)

    def row_of(i):
        return lax.rem(x + i, X)

    def exchange_copy(exchange, i, j, outward):
        send, recv, sems = exchange
        k = i * Z + j
        if outward:
            peer = lax.rem(x + X - i, X) * Z + lax.rem(z + j, Z)
            return remote(send.at[peer], recv.at[s], S[sems + "_s"].at[k], S[sems + "_r"].at[k], (peer, e))
        peer = row_of(i) * Z + lax.rem(z + Z - j, Z)
        return remote(send.at[peer], recv.at[peer], S[sems + "_s"].at[k], S[sems + "_r"].at[k], (peer, e))

    def each_peer(i, act):
        def go(j, carry):
            act(j)
            return carry

        lax.fori_loop(1 if i == 0 else 0, Z, go, 0)

    def exchange_send(exchange, i):
        if i == 0:
            exchange[1][s] = exchange[0][s]
        each_peer(i, lambda j: exchange_copy(exchange, i, j, True).start())

    def exchange_wait(exchange, i):
        each_peer(i, lambda j: exchange_copy(exchange, i, j, False).wait_recv())

    def exchange_drain(exchange):
        for i in range(X):
            each_peer(i, lambda j: exchange_copy(exchange, i, j, True).wait_send())

    grad_exchange = (S["gs"], S["gr"], "sem_ga")
    token_exchange = (S["ts"], S["tr"], "sem_ta")
    back_exchange = (S["bs"], S["br"], "sem_ba")
    spread(S["gs"], nt(S["routing"][...], scaled.astype(BF16)))
    pl.semaphore_wait(S["columns_in"], X - 1)
    for i in range(X):
        exchange_send(grad_exchange, i)
    drains.append(lambda: exchange_drain(grad_exchange))

    per_part, padded_part = R // X, RP // X

    def packed_of(index):
        block = (index * (65536 // PAD + 1)) >> 16
        inner = index - block * PAD
        return jnp.where(inner < CAP, block * CAP + inner, -1)

    S["comp"][...] = jnp.where(
        lax.broadcasted_iota(jnp.int32, (per_part, padded_part), 0)
        == packed_of(lax.broadcasted_iota(jnp.int32, (per_part, padded_part), 1)),
        1.0,
        0.0,
    ).astype(BF16)
    S["compt"][...] = jnp.where(
        packed_of(lax.broadcasted_iota(jnp.int32, (padded_part, per_part), 0))
        == lax.broadcasted_iota(jnp.int32, (padded_part, per_part), 1),
        1.0,
        0.0,
    ).astype(BF16)

    def part_rows(i):
        align = 16 if per_part % 16 == 0 else 1
        return pl.ds(pl.multiple_of(row_of(i) * per_part, align), per_part)

    def pack(exchange, buf, i):
        part = exchange[1][pl.ds(row_of(i) * Z, Z)].astype(F32).reshape(padded_part, HD)
        buf[e, part_rows(i), :] = nn(S["comp"][...], part.astype(BF16)).astype(BF16)

    slope = slope_ref[0]
    S["cb"][...] = lax.broadcasted_iota(jnp.int32, (BL, BL), 0).astype(F32) * slope
    causal = lax.broadcasted_iota(jnp.int32, (BL, BL), 0) <= lax.broadcasted_iota(
        jnp.int32, (BL, BL), 1
    )

    def pieces(d, j):
        def offset(r):
            distance = ((j - z) * BL).astype(F32) + float(r * Z * BL)
            return jnp.where(x >= r, 0.0, NEG) - slope * distance

        if d == 0:
            return [(0, offset(0), causal), (1, offset(1), None), (2, offset(2), ~causal)]
        r = jnp.where(j > z, 0, 2)
        near = jnp.where(j > z, offset(0), offset(2))
        return [(r, near, None), (1, offset(1), None)]

    def scores_of(r, offset, mask, queries):
        raw = nt(S["k3"][r], queries) * scale + (S["cb"][...] + offset)
        return raw if mask is None else jnp.where(mask, raw, NEG)

    def forward(d):
        j = lax.rem(z + d, Z)
        queries = S["qb"][j]
        parts = pieces(d, j)
        scores = [scores_of(r, offset, mask, queries) for r, offset, mask in parts]
        top = functools.reduce(
            jnp.maximum, [jnp.max(t, axis=0, keepdims=True) for t in scores]
        )
        total, out = 0.0, 0.0
        for (r, _, _), t in zip(parts, scores):
            p = jnp.exp(t - top)
            total = total + jnp.sum(p, axis=0, keepdims=True)
            out = out + nn(S["vt3"][r], p.astype(BF16))
        out = (out / total).astype(BF16)
        log_norm = top + jnp.log(total)
        if d == 0:
            S["orecv"][0] = out
            S["lrecv"][0] = log_norm
            return
        S["osend"][d] = out
        S["lsend"][d] = log_norm
        out_copy(d).start()
        norm_copy(d).start()
        drains.append(out_copy(d).wait_send)
        drains.append(norm_copy(d).wait_send)

    def out_copy(d):
        return remote(S["osend"].at[d], S["orecv"].at[d], S["sem_o_s"].at[d], S["sem_o_r"].at[d],
                      zdev(lax.rem(z + d, Z)))

    def norm_copy(d):
        return remote(S["lsend"].at[d], S["lrecv"].at[d], S["sem_l_s"].at[d], S["sem_l_r"].at[d],
                      zdev(lax.rem(z + d, Z)))

    def feature_view(buf, block, core, part):
        return buf.at[2 * block + core, part_rows(part), :]

    def feature_ring(buf, ring, sib):
        def arrived(block, distance, part):
            sib_copy(buf, sib, block, distance, part, c).start()

        return GatherRing(
            Y, X, y, ydev, lambda b, p: feature_view(buf, b, c, p),
            [S["sem_" + ring + end] for end in ("_rs", "_rr", "_ls", "_lr")], arrived,
        )

    def sib_copy(buf, sib, block, distance, part, core):
        ref = feature_view(buf, block, core, part)
        i = X * distance + part
        return remote(ref, ref, S["sem_" + sib + "_s"].at[i], S["sem_" + sib + "_r"].at[i], sibling)

    def sib_wait(buf, sib, distance):
        for part in range(X):
            sib_copy(buf, sib, lax.rem(y + distance, Y), distance, part, 1 - c).wait_recv()

    def sib_drain(buf, sib):
        for distance in range(Y):
            for part in range(X):
                sib_copy(buf, sib, lax.rem(y + distance, Y), distance, part, c).wait_send()

    def ring_from_exchange(exchange, buf, ring):
        for i in range(X):
            exchange_wait(exchange, i)
            pack(exchange, buf, i)
            ring.start(i)

    grad_ring = feature_ring(S["grads"], "ygr", "gsib")
    drains.append(grad_ring.drain)
    drains.append(lambda: sib_drain(S["grads"], "gsib"))
    y_half, z_half = Y // 2, Z // 2
    grad_hops = list(range(y_half + 1))

    def advance_grads():
        if not grad_hops:
            return
        k = grad_hops.pop(0)
        if k == 0:
            ring_from_exchange(grad_exchange, S["grads"], grad_ring)
        else:
            for part in range(X):
                grad_ring.step(k, part)

    def neighbours(k, n):
        return [0] if k == 0 else sorted({k, n - k})

    for k in range(1, z_half + 2):
        if k <= z_half:
            for part in range(2):
                q_ring.step(k, part)
        if k == 1:
            S["kt3"][0] = transposed(k_ref[...])
            S["vt3"][0] = transposed(v_ref[...])
            for copy in kv_copies:
                copy.wait_recv()
            for r in (1, 2):
                S["kt3"][r] = transposed(S["k3"][r])
                S["vt3"][r] = transposed(S["v3"][r])
        for d in neighbours(k - 1, Z):
            forward(d)
        if k >= 2 and k <= z_half:
            advance_grads()
    advance_grads()

    for d in range(1, Z):
        out_copy(d).wait_recv()
        norm_copy(d).wait_recv()
    norms = [S["lrecv"][d][0:1, :] for d in range(Z)]
    top = functools.reduce(jnp.maximum, norms)
    shares = [jnp.exp(t - top) for t in norms]
    total = functools.reduce(jnp.add, shares)
    merged = functools.reduce(
        jnp.add, [S["orecv"][d].astype(F32) * shares[d] for d in range(Z)]
    )
    out_t = (merged / total).astype(BF16)
    S["ot"][...] = out_t
    log_norm = top + jnp.log(total)
    S["stats"][z, 0:1, :] = log_norm

    spread(S["ts"], nt(S["routing"][...], jnp.concatenate([out_t, out_t], axis=1)))
    for i in range(X):
        exchange_send(token_exchange, i)
    drains.append(lambda: exchange_drain(token_exchange))

    def pair(buf, block):
        return jnp.concatenate([buf[2 * block], buf[2 * block + 1]], axis=1)

    def columns(block):
        return pl.ds(pl.multiple_of(block * (2 * HD), 2 * HD), 2 * HD)

    order = [0]
    for k in range(1, Y // 2 + 1):
        order += sorted({k, Y - k})

    for copy in weights_in:
        copy.wait()
    while grad_hops:
        advance_grads()
    for n, d in enumerate(order):
        sib_wait(S["grads"], "gsib", d)
        block = lax.rem(y + d, Y)
        term = nt(pair(S["grads"], block), S["wout"][:, columns(block)])
        S["thr"][...] = term if n == 0 else S["thr"][...] + term

    token_ring = feature_ring(S["toks"], "ytk", "tsib")
    drains.append(token_ring.drain)
    drains.append(lambda: sib_drain(S["toks"], "tsib"))
    ring_from_exchange(token_exchange, S["toks"], token_ring)

    def pre_term(d):
        sib_wait(S["toks"], "tsib", d)
        block = lax.rem(y + d, Y)
        term = nn(pair(S["toks"], block), S["win"][columns(block), :])
        S["pre"][...] = term if d == 0 else S["pre"][...] + term

    for k in range(1, y_half + 2):
        if k <= y_half:
            for part in range(X):
                token_ring.step(k, part)
        for d in neighbours(k - 1, Y):
            pre_term(d)

    pre = S["pre"][...]
    logistic = 1.0 / (1.0 + jnp.exp(-pre))
    S["hid"][...] = jnp.transpose(pre * logistic).astype(BF16)
    S["hg"][...] = (S["thr"][...] * logistic * (1.0 + pre * (1.0 - logistic))).astype(BF16)

    def partner_copy(distance):
        block = lax.rem(y + distance, Y)
        return remote(S["sb"].at[block], S["rb"].at[block], S["sem_psib_s"].at[distance],
                      S["sem_psib_r"].at[distance], sibling)

    far_first = order[::-1]
    for d in far_first:
        block = lax.rem(y + d, Y)
        share = nt(S["hg"][...], S["win"][columns(block), :]).astype(BF16)
        first, second = share[:, :HD], share[:, HD:]
        S["pb"][block] = jnp.where(c == 0, first, second)
        S["sb"][block] = jnp.where(c == 0, second, first)
        partner_copy(d).start()
        drains.append(partner_copy(d).wait_send)

    half = y_half

    def hops(direction, chunk):
        return half if (chunk < X // 2) == (direction == 0) else half - 1

    def ring_copy(direction, chunk, h):
        i = X * h + chunk
        ends = ("_rs", "_rr") if direction == 0 else ("_ls", "_lr")
        neighbour = ydev(lax.rem(y + 1, Y)) if direction == 0 else ydev(lax.rem(y + Y - 1, Y))
        return remote(S["rs_stage"].at[direction, i], S["rs_recv"].at[direction, i],
                      S["sem_rs" + ends[0]].at[i], S["sem_rs" + ends[1]].at[i], neighbour)

    def own_part(block, chunk):
        span = part_rows(chunk)
        return S["pb"][block, span, :].astype(F32) + S["rb"][block, span, :].astype(F32)

    lanes = [(0, i) for i in range(X)] + [(1, (i + X // 2) % X) for i in range(X)]
    lanes = [lane for both in zip(lanes[:X], lanes[X:]) for lane in both]

    weight_work = [("out", d) for d in order] + [("in", d) for d in order]

    def some_weight_work(count):
        for _ in range(min(count, len(weight_work))):
            which, d = weight_work.pop(0)
            block = lax.rem(y + d, Y)
            if which == "out":
                S["dwo"][:, columns(block)] = nn(S["hid"][...], pair(S["grads"], block)).astype(BF16)
            else:
                S["dwi"][columns(block), :] = tn(pair(S["toks"], block), S["hg"][...]).astype(BF16)

    waited = set()

    def need_partner(distance):
        if distance not in waited:
            waited.add(distance)
            partner_copy(distance).wait_recv()

    per_hop = -(-2 * Y // half)
    for h in range(half):
        for direction, chunk in lanes:
            total_hops = hops(direction, chunk)
            if h >= total_hops:
                continue
            distance = total_hops - h if direction == 0 else Y - (total_hops - h)
            need_partner(distance)
            value = own_part(lax.rem(y + distance, Y), chunk)
            if h > 0:
                ring_copy(direction, chunk, h - 1).wait_recv()
                value = value + S["rs_recv"][direction, X * (h - 1) + chunk].astype(F32)
            S["rs_stage"][direction, X * h + chunk] = value.astype(BF16)
            ring_copy(direction, chunk, h).start()
            drains.append(ring_copy(direction, chunk, h).wait_send)
        some_weight_work(per_hop)
    need_partner(0)
    for chunk in range(X):
        value = own_part(y, chunk)
        for direction in range(2):
            last = hops(direction, chunk) - 1
            if last >= 0:
                ring_copy(direction, chunk, last).wait_recv()
                value = value + S["rs_recv"][direction, X * last + chunk].astype(F32)
        padded = nn(S["compt"][...], value.astype(BF16)).reshape(Z, PAD, HD)
        S["bs"][pl.ds(row_of(chunk) * Z, Z)] = padded.astype(BF16)
        exchange_send(back_exchange, (X - chunk) % X)
    drains.append(lambda: exchange_drain(back_exchange))
    some_weight_work(2 * Y)
    weights_out = [
        pltpu.make_async_copy(S["dwi"], dwi_ref.at[0], S["sem_dw"].at[0]),
        pltpu.make_async_copy(S["dwo"], dwo_ref.at[0], S["sem_dw"].at[1]),
    ]
    for copy in weights_out:
        copy.start()
        drains.append(copy.wait)
    for i in range(X):
        exchange_wait(back_exchange, i)
    returned = S["br"][...].astype(F32).reshape(RP, HD).astype(BF16)
    combined = tn(returned, S["routing"][...])
    grad_t = (S["ogt"][...] + combined[:, :BL] + combined[:, BL:]).astype(BF16).astype(F32)
    delta = jnp.sum(grad_t * S["ot"][...].astype(F32), axis=0, keepdims=True)
    S["stats"][z, 1:2, :] = delta
    S["gb"][z] = jnp.transpose(grad_t).astype(BF16)

    g_ring = GatherRing(
        Z, 2, z, zdev, lambda b, p: S["gb"].at[b, pl.ds(p * (BL // 2), BL // 2), :],
        [S["sem_g_rs"], S["sem_g_rr"], S["sem_g_ls"], S["sem_g_lr"]],
    )

    def stats_copy(d, block):
        ref = S["stats"].at[block]
        return remote(ref, ref, S["sem_st_s"].at[d], S["sem_st_r"].at[d], zdev(lax.rem(z + d, Z)))

    for part in range(2):
        g_ring.start(part)
    drains.append(g_ring.drain)
    for d in range(1, Z):
        stats_copy(d, z).start()
        drains.append(stats_copy(d, z).wait_send)

    def dq_copy(d):
        return remote(S["dqsend"].at[d], S["dqrecv"].at[d], S["sem_dq_s"].at[d], S["sem_dq_r"].at[d],
                      zdev(lax.rem(z + d, Z)))

    def backward(d):
        j = lax.rem(z + d, Z)
        queries, grads = S["qb"][j], S["gb"][j]
        norm, dlt = S["stats"][j, 0:1, :], S["stats"][j, 1:2, :]
        dq = 0.0
        for r, offset, mask in pieces(d, j):
            p = jnp.exp(scores_of(r, offset, mask, queries) - norm)
            dv = nn(p.astype(BF16), grads)
            ds = (p * (nt(S["v3"][r], grads) - dlt)).astype(BF16)
            dk = nn(ds, queries)
            dq = dq + nn(S["kt3"][r], ds)
            if d == 0:
                S["dv3"][r], S["dk3"][r] = dv, dk
            else:
                S["dv3"][r] = S["dv3"][r] + dv
                S["dk3"][r] = S["dk3"][r] + dk
        dq = dq * scale
        if d == 0:
            S["dqown"][...] = dq
        else:
            S["dqsend"][d] = dq.astype(BF16)
            dq_copy(d).start()
            drains.append(dq_copy(d).wait_send)

    for k in range(1, z_half + 2):
        if k <= z_half:
            for part in range(2):
                g_ring.step(k, part)
        for d in neighbours(k - 1, Z):
            if d:
                stats_copy(Z - d, lax.rem(z + d, Z)).wait_recv()
            backward(d)

    dkv_copies = []
    for hop in (1, 2):
        S["dksend"][hop - 1] = (S["dk3"][hop] * scale).astype(BF16)
        S["dvsend"][hop - 1] = S["dv3"][hop].astype(BF16)
        for which, name in enumerate(("dk", "dv")):
            i = 2 * (hop - 1) + which
            copy = remote(S[name + "send"].at[hop - 1], S[name + "recv"].at[hop - 1],
                          S["sem_dkv_s"].at[i], S["sem_dkv_r"].at[i], xdev(x + X - hop))
            copy.start()
            dkv_copies.append(copy)
            drains.append(copy.wait_send)

    dq = S["dqown"][...]
    for d in range(1, Z):
        dq_copy(d).wait_recv()
        dq = dq + S["dqrecv"][d].astype(F32)
    dq_ref[...] = jnp.transpose(dq).astype(BF16)
    for copy in dkv_copies:
        copy.wait_recv()
    dk_ref[...] = (
        S["dk3"][0] * scale + S["dkrecv"][0].astype(F32) + S["dkrecv"][1].astype(F32)
    ).astype(BF16)
    dv_ref[...] = (
        S["dv3"][0] + S["dvrecv"][0].astype(F32) + S["dvrecv"][1].astype(F32)
    ).astype(BF16)

    for f in drains:
        f()


def hand_over(*refs):
    sems = refs[10]
    copies = [pltpu.make_async_copy(refs[i], refs[5 + i], sems.at[i]) for i in range(5)]
    for copy in copies:
        copy.start()
    for copy in copies:
        copy.wait()


def per_device(
    queries,
    key_rows,
    value_rows,
    out_grad,
    expert_ids,
    gate_values,
    alibi_slope,
    expert_in,
    expert_out,
):
    E, N = lax.axis_size("seq"), lax.axis_size("exp")
    Y, Z = N // 2, WCH // 2
    BL = queries.shape[0]
    D, FL = expert_in.shape[1:]
    CAP = 5 * BL // (2 * E)
    scratch = scratch_table(E, Y, Z, BL, D, FL, CAP)
    vmem = pl.BlockSpec(memory_space=pltpu.VMEM)
    smem = pl.BlockSpec(memory_space=pltpu.SMEM)
    hbm = pl.BlockSpec(memory_space=pl.ANY)
    shape = jax.ShapeDtypeStruct
    outs = pl.pallas_call(
        functools.partial(body, list(scratch), E, Y, Z, CAP),
        out_shape=(
            shape(queries.shape, BF16),
            shape(queries.shape, BF16),
            shape(queries.shape, BF16),
            shape(expert_in.shape, BF16),
            shape(expert_out.shape, BF16),
        ),
        in_specs=[vmem] * 6 + [smem] + [hbm] * 2,
        out_specs=(vmem, vmem, vmem, hbm, hbm),
        scratch_shapes=list(scratch.values()),
        compiler_params=pltpu.CompilerParams(
            collective_id=0, has_side_effects=True, vmem_limit_bytes=56 * 2**20
        ),
    )(
        queries,
        key_rows,
        value_rows,
        out_grad,
        expert_ids.T,
        gate_values.T,
        alibi_slope,
        expert_in,
        expert_out,
    )
    return pl.pallas_call(
        hand_over,
        out_shape=tuple(shape(out.shape, out.dtype) for out in outs),
        in_specs=[hbm] * 5,
        out_specs=(hbm,) * 5,
        scratch_shapes=[pltpu.SemaphoreType.DMA((5,))],
    )(*outs)


def solution(mesh):
    return jax.shard_map(
        per_device,
        mesh=mesh,
        in_specs=(
            P("seq", "exp"),
            P("seq", "exp"),
            P("seq", "exp"),
            P("seq", "exp"),
            P("seq", None),
            P("seq", None),
            P("exp"),
            P("seq", None, "exp"),
            P("seq", "exp", None),
        ),
        out_specs=(
            P("seq", "exp"),
            P("seq", "exp"),
            P("seq", "exp"),
            P("seq", None, "exp"),
            P("seq", "exp", None),
        ),
        check_vma=False,
    )
```

```python
import functools

import jax
import jax.numpy as jnp
from jax import lax
from jax.experimental import pallas as pl
from jax.experimental.pallas import tpu as pltpu
from jax.sharding import PartitionSpec as P

HD = 128
WCH = 16
PAD = 24
F32 = jnp.float32
BF16 = jnp.bfloat16
MESH = pl.DeviceIdType.MESH
NEG = -1.0e30


def nt(a, b):
    return lax.dot_general(a, b, (((1,), (1,)), ((), ())), preferred_element_type=F32)


def nn(a, b):
    return lax.dot_general(a, b, (((1,), (0,)), ((), ())), preferred_element_type=F32)


def tn(a, b):
    return lax.dot_general(a, b, (((0,), (0,)), ((), ())), preferred_element_type=F32)


def transposed(a):
    return jnp.transpose(a.astype(F32)).astype(BF16)


def remote(src, dst, send_sem, recv_sem, device):
    return pltpu.make_async_remote_copy(
        src_ref=src,
        dst_ref=dst,
        send_sem=send_sem,
        recv_sem=recv_sem,
        device_id=device,
        device_id_type=MESH,
    )


class GatherRing:
    def __init__(self, count, parts, me, device_of, view, sems):
        self.n, self.parts, self.me, self.view = count, parts, me, view
        self.half = count // 2
        self.right = device_of(lax.rem(me + 1, count))
        self.left = device_of(lax.rem(me + count - 1, count))
        self.sems = sems

    def block(self, direction, hops):
        return lax.rem(self.me + (self.n - hops if direction == 0 else hops), self.n)

    def sends(self, direction, k, part):
        return k < self.half - 1 or (k == self.half - 1 and self.ahead(direction, part))

    def ahead(self, direction, part):
        return (part < self.parts // 2) == (direction == 0)

    def copy(self, direction, k, part, hops):
        ref = self.view(self.block(direction, hops), part)
        i = self.parts * k + part
        return remote(
            ref,
            ref,
            self.sems[2 * direction].at[i],
            self.sems[2 * direction + 1].at[i],
            self.right if direction == 0 else self.left,
        )

    def start(self, part):
        for direction in range(2):
            if self.sends(direction, 0, part):
                self.copy(direction, 0, part, 0).start()

    def step(self, k, part):
        for direction in range(2):
            if not self.sends(direction, k - 1, part):
                continue
            self.copy(direction, k - 1, part, k).wait_recv()
            if self.sends(direction, k, part):
                self.copy(direction, k, part, k).start()

    def drain(self):
        for k in range(self.half):
            for part in range(self.parts):
                for direction in range(2):
                    if self.sends(direction, k, part):
                        self.copy(direction, k, part, k).wait_send()


def scratch_table(E, Y, Z, BL, D, FL, CAP):
    R, RP, hz, hy, X = E * CAP, E * PAD, max(Z // 2, 1), max(Y // 2, 1), E // Z
    table = dict(
        k3=((3, BL, HD), BF16),
        v3=((3, BL, HD), BF16),
        kt3=((3, HD, BL), BF16),
        vt3=((3, HD, BL), BF16),
        qb=((Z, BL, HD), BF16),
        gb=((Z, BL, HD), BF16),
        cb=((BL, BL), F32),
        osend=((Z, HD, BL), BF16),
        orecv=((Z, HD, BL), BF16),
        lsend=((Z, 1, BL), F32),
        lrecv=((Z, 1, BL), F32),
        stats=((Z, 2, BL), F32),
        ot=((HD, BL), BF16),
        ogt=((HD, BL), F32),
        routing=((RP, 2 * BL), BF16),
        comp=((R // X, RP // X), BF16),
        compt=((RP // X, R // X), BF16),
        gs=((E, PAD, HD), BF16),
        gr=((E, PAD, HD), BF16),
        ts=((E, PAD, HD), BF16),
        tr=((E, PAD, HD), BF16),
        bs=((E, PAD, HD), BF16),
        br=((E, PAD, HD), BF16),
        grads=((2 * Y, R, HD), BF16),
        toks=((2 * Y, R, HD), BF16),
        win=((D, FL), BF16),
        wout=((FL, D), BF16),
        thr=((R, FL), F32),
        pre=((R, FL), F32),
        hid=((FL, R), BF16),
        hg=((R, FL), BF16),
        pb=((Y, R, HD), BF16),
        sb=((Y, R, HD), BF16),
        rb=((Y, R, HD), BF16),
        rs_stage=((2, X * hy, R // X, HD), BF16),
        rs_recv=((2, X * hy, R // X, HD), BF16),
        dk3=((3, BL, HD), F32),
        dv3=((3, BL, HD), F32),
        dksend=((2, BL, HD), BF16),
        dvsend=((2, BL, HD), BF16),
        dkrecv=((2, BL, HD), BF16),
        dvrecv=((2, BL, HD), BF16),
        dqsend=((Z, HD, BL), BF16),
        dqrecv=((Z, HD, BL), BF16),
        dqown=((HD, BL), F32),
    )
    shapes = {name: pltpu.VMEM(shape, dtype) for name, (shape, dtype) in table.items()}
    counts = dict(
        kv_s=4, kv_r=4, o_s=Z, o_r=Z, l_s=Z, l_r=Z, st_s=Z, st_r=Z, dq_s=Z, dq_r=Z, dkv_s=4, dkv_r=4,
        ga_s=E, ga_r=E, ta_s=E, ta_r=E, ba_s=E, ba_r=E, w=2,
        gsib_s=X * Y, gsib_r=X * Y, tsib_s=X * Y, tsib_r=X * Y, psib_s=Y, psib_r=Y,
    )
    for ring, half in (("q", 2 * hz), ("g", 2 * hz), ("ygr", X * hy), ("ytk", X * hy), ("rs", X * hy)):
        for end in ("_rs", "_rr", "_ls", "_lr"):
            counts[ring + end] = half
    for name, count in counts.items():
        shapes["sem_" + name] = pltpu.SemaphoreType.DMA((count,))
    shapes["columns_in"] = pltpu.SemaphoreType.REGULAR
    return shapes


def body(names, E, Y, Z, CAP, *refs):
    (q_ref, k_ref, v_ref, og_ref, ids_ref, gates_ref, slope_ref, win_ref, wout_ref,
     dq_ref, dk_ref, dv_ref, dwi_ref, dwo_ref) = refs[:14]
    S = dict(zip(names, refs[14:]))
    BL, FL = q_ref.shape[0], win_ref.shape[2]
    X, R, RP, D = E // Z, E * CAP, E * PAD, 2 * Y * HD
    scale = HD ** (-0.5)
    s, e = lax.axis_index("seq"), lax.axis_index("exp")
    x, z = lax.div(s, Z), lax.rem(s, Z)
    y, c = lax.div(e, 2), lax.rem(e, 2)
    sibling = (s, 2 * y + 1 - c)

    def zdev(j):
        return (x * Z + j, e)

    def xdev(i):
        return (lax.rem(i, X) * Z + z, e)

    def ydev(j):
        return (s, 2 * j + c)

    drains = []
    barrier = pltpu.get_barrier_semaphore()
    near = [zdev(lax.rem(z + d, Z)) for d in range(1, Z)] + [xdev(x + d) for d in range(1, X)]
    near += [ydev(lax.rem(y + 1, Y)), ydev(lax.rem(y + Y - 1, Y)), sibling]
    for device in near:
        pl.semaphore_signal(barrier, inc=1, device_id=device, device_id_type=MESH)

    weights_in = [
        pltpu.make_async_copy(win_ref.at[0], S["win"], S["sem_w"].at[0]),
        pltpu.make_async_copy(wout_ref.at[0], S["wout"], S["sem_w"].at[1]),
    ]
    for copy in weights_in:
        copy.start()
    S["qb"][z] = q_ref[...]
    S["k3"][0] = k_ref[...]
    S["v3"][0] = v_ref[...]
    pl.semaphore_wait(barrier, len(near))

    q_ring = GatherRing(
        Z, 2, z, zdev, lambda b, p: S["qb"].at[b, pl.ds(p * (BL // 2), BL // 2), :],
        [S["sem_q_rs"], S["sem_q_rr"], S["sem_q_ls"], S["sem_q_lr"]],
    )
    for part in range(2):
        q_ring.start(part)
    drains.append(q_ring.drain)
    kv_copies = []
    for hop in (1, 2):
        for which, (own, buf) in enumerate((("k3", "k3"), ("v3", "v3"))):
            i = 2 * (hop - 1) + which
            copy = remote(
                S[own].at[0], S[buf].at[hop], S["sem_kv_s"].at[i], S["sem_kv_r"].at[i],
                xdev(x + hop),
            )
            copy.start()
            kv_copies.append(copy)
            drains.append(copy.wait_send)

    y_half, z_half = Y // 2, Z // 2
    query_hops = list(range(1, z_half + 1))

    def take_queries(upto):
        while query_hops and query_hops[0] <= upto:
            k = query_hops.pop(0)
            for part in range(2):
                q_ring.step(k, part)

    for d in range(1, X):
        pl.semaphore_signal(
            S["columns_in"], inc=1, device_id=xdev(x + d), device_id_type=MESH
        )

    flat = jnp.concatenate([ids_ref[0:1, :], ids_ref[1:2, :]], axis=1)
    hot = lax.broadcasted_iota(jnp.int32, (E, 2 * BL), 0) == flat
    hot_f = jnp.where(hot, 1.0, 0.0)
    upper = lax.broadcasted_iota(jnp.int32, (2 * BL, 2 * BL), 0) < lax.broadcasted_iota(
        jnp.int32, (2 * BL, 2 * BL), 1
    )
    before = nn(hot_f.astype(BF16), jnp.where(upper, 1.0, 0.0).astype(BF16))
    position = jnp.sum(before * hot_f, axis=0, keepdims=True)
    slot = jnp.where(position < CAP, flat * PAD + position.astype(jnp.int32), -1)
    S["routing"][...] = jnp.where(
        lax.broadcasted_iota(jnp.int32, (RP, 2 * BL), 0) == slot, 1.0, 0.0
    ).astype(BF16)
    ogt = jnp.transpose(og_ref[...].astype(F32))
    S["ogt"][...] = ogt
    scaled = jnp.concatenate([ogt * gates_ref[0:1, :], ogt * gates_ref[1:2, :]], axis=1)
    def spread(send, value):
        send[...] = value.reshape(E, PAD, HD).astype(BF16)

    def row_of(i):
        return lax.rem(x + i, X)

    def exchange_copy(exchange, i, j, outward):
        send, recv, sems = exchange
        k = i * Z + j
        if outward:
            peer = lax.rem(x + X - i, X) * Z + lax.rem(z + j, Z)
            return remote(send.at[peer], recv.at[s], S[sems + "_s"].at[k], S[sems + "_r"].at[k], (peer, e))
        peer = row_of(i) * Z + lax.rem(z + Z - j, Z)
        return remote(send.at[peer], recv.at[peer], S[sems + "_s"].at[k], S[sems + "_r"].at[k], (peer, e))

    def each_peer(i, act):
        def go(j, carry):
            act(j)
            return carry

        lax.fori_loop(1 if i == 0 else 0, Z, go, 0)

    def exchange_send(exchange, i):
        if i == 0:
            exchange[1][s] = exchange[0][s]
        each_peer(i, lambda j: exchange_copy(exchange, i, j, True).start())

    def exchange_wait(exchange, i):
        each_peer(i, lambda j: exchange_copy(exchange, i, j, False).wait_recv())

    def exchange_drain(exchange):
        for i in range(X):
            each_peer(i, lambda j: exchange_copy(exchange, i, j, True).wait_send())

    grad_exchange = (S["gs"], S["gr"], "sem_ga")
    token_exchange = (S["ts"], S["tr"], "sem_ta")
    back_exchange = (S["bs"], S["br"], "sem_ba")
    spread(S["gs"], nt(S["routing"][...], scaled.astype(BF16)))
    take_queries(1)
    pl.semaphore_wait(S["columns_in"], X - 1)
    for i in range(X):
        exchange_send(grad_exchange, i)
    drains.append(lambda: exchange_drain(grad_exchange))
    take_queries(2)

    per_part, padded_part = R // X, RP // X

    def packed_of(index):
        block = (index * (65536 // PAD + 1)) >> 16
        inner = index - block * PAD
        return jnp.where(inner < CAP, block * CAP + inner, -1)

    S["comp"][...] = jnp.where(
        lax.broadcasted_iota(jnp.int32, (per_part, padded_part), 0)
        == packed_of(lax.broadcasted_iota(jnp.int32, (per_part, padded_part), 1)),
        1.0,
        0.0,
    ).astype(BF16)
    S["compt"][...] = jnp.where(
        packed_of(lax.broadcasted_iota(jnp.int32, (padded_part, per_part), 0))
        == lax.broadcasted_iota(jnp.int32, (padded_part, per_part), 1),
        1.0,
        0.0,
    ).astype(BF16)

    def part_rows(i):
        align = 16 if per_part % 16 == 0 else 1
        return pl.ds(pl.multiple_of(row_of(i) * per_part, align), per_part)

    def pack(exchange, buf, i):
        part = exchange[1][pl.ds(row_of(i) * Z, Z)].astype(F32).reshape(padded_part, HD)
        buf[e, part_rows(i), :] = nn(S["comp"][...], part.astype(BF16)).astype(BF16)

    slope = slope_ref[0]
    S["cb"][...] = lax.broadcasted_iota(jnp.int32, (BL, BL), 0).astype(F32) * slope
    causal = lax.broadcasted_iota(jnp.int32, (BL, BL), 0) <= lax.broadcasted_iota(
        jnp.int32, (BL, BL), 1
    )

    def pieces(d, j):
        def offset(r):
            distance = ((j - z) * BL).astype(F32) + float(r * Z * BL)
            return jnp.where(x >= r, 0.0, NEG) - slope * distance

        if d == 0:
            return [(0, offset(0), causal), (1, offset(1), None), (2, offset(2), ~causal)]
        r = jnp.where(j > z, 0, 2)
        near = jnp.where(j > z, offset(0), offset(2))
        return [(r, near, None), (1, offset(1), None)]

    def scores_of(r, offset, mask, queries):
        raw = nt(S["k3"][r], queries) * scale + (S["cb"][...] + offset)
        return raw if mask is None else jnp.where(mask, raw, NEG)

    def forward(d):
        j = lax.rem(z + d, Z)
        queries = S["qb"][j]
        parts = pieces(d, j)
        scores = [scores_of(r, offset, mask, queries) for r, offset, mask in parts]
        top = functools.reduce(
            jnp.maximum, [jnp.max(t, axis=0, keepdims=True) for t in scores]
        )
        total, out = 0.0, 0.0
        for (r, _, _), t in zip(parts, scores):
            p = jnp.exp(t - top)
            total = total + jnp.sum(p, axis=0, keepdims=True)
            out = out + nn(S["vt3"][r], p.astype(BF16))
        out = (out / total).astype(BF16)
        log_norm = top + jnp.log(total)
        if d == 0:
            S["orecv"][0] = out
            S["lrecv"][0] = log_norm
            return
        S["osend"][d] = out
        S["lsend"][d] = log_norm
        out_copy(d).start()
        norm_copy(d).start()
        drains.append(out_copy(d).wait_send)
        drains.append(norm_copy(d).wait_send)

    def out_copy(d):
        return remote(S["osend"].at[d], S["orecv"].at[d], S["sem_o_s"].at[d], S["sem_o_r"].at[d],
                      zdev(lax.rem(z + d, Z)))

    def norm_copy(d):
        return remote(S["lsend"].at[d], S["lrecv"].at[d], S["sem_l_s"].at[d], S["sem_l_r"].at[d],
                      zdev(lax.rem(z + d, Z)))

    def feature_view(buf, block, core, part):
        return buf.at[2 * block + core, part_rows(part), :]

    def feature_ring(buf, ring):
        return GatherRing(
            Y, X, y, ydev, lambda b, p: feature_view(buf, b, c, p),
            [S["sem_" + ring + end] for end in ("_rs", "_rr", "_ls", "_lr")],
        )

    def sib_copies(buf, sib, distance, core):
        block = 2 * lax.rem(y + distance, Y) + core
        refs = [buf.at[block]]
        if distance == y_half:
            refs = [buf.at[block, part_rows(part), :] for part in range(X)]
        return [
            remote(ref, ref, S["sem_" + sib + "_s"].at[distance + Y * n],
                   S["sem_" + sib + "_r"].at[distance + Y * n], sibling)
            for n, ref in enumerate(refs)
        ]

    def sib_send(buf, sib, k):
        for distance in neighbours(k, Y):
            for copy in sib_copies(buf, sib, distance, c):
                copy.start()

    def sib_wait(buf, sib, distance):
        for copy in sib_copies(buf, sib, distance, 1 - c):
            copy.wait_recv()

    def sib_drain(buf, sib):
        for distance in range(Y):
            for copy in sib_copies(buf, sib, distance, c):
                copy.wait_send()

    def ring_hop(ring, buf, sib, k):
        for part in range(X):
            ring.step(k, part)
            if k == y_half:
                sib_copies(buf, sib, k, c)[part].start()
        if k < y_half:
            sib_send(buf, sib, k)

    def neighbours(k, n):
        return [0] if k == 0 else sorted({k, n - k})

    def ring_from_exchange(exchange, buf, ring, sib):
        for i in range(X):
            exchange_wait(exchange, i)
            pack(exchange, buf, i)
            ring.start(i)
        sib_send(buf, sib, 0)

    grad_ring = feature_ring(S["grads"], "ygr")
    drains.append(grad_ring.drain)
    drains.append(lambda: sib_drain(S["grads"], "gsib"))
    grad_hops = list(range(y_half + 1))

    def advance_grads():
        if not grad_hops:
            return
        k = grad_hops.pop(0)
        if k == 0:
            ring_from_exchange(grad_exchange, S["grads"], grad_ring, "gsib")
        else:
            ring_hop(grad_ring, S["grads"], "gsib", k)

    S["kt3"][0] = transposed(k_ref[...])
    S["vt3"][0] = transposed(v_ref[...])
    for copy in kv_copies:
        copy.wait_recv()
    for r in (1, 2):
        S["kt3"][r] = transposed(S["k3"][r])
        S["vt3"][r] = transposed(S["v3"][r])
    forward(0)
    take_queries(3)
    for k in range(1, z_half + 1):
        if k == z_half:
            take_queries(k)
        for d in neighbours(k, Z):
            forward(d)
        if k != 2:
            advance_grads()

    for d in range(1, Z):
        out_copy(d).wait_recv()
        norm_copy(d).wait_recv()
    norms = [S["lrecv"][d][0:1, :] for d in range(Z)]
    top = functools.reduce(jnp.maximum, norms)
    shares = [jnp.exp(t - top) for t in norms]
    total = functools.reduce(jnp.add, shares)
    merged = functools.reduce(
        jnp.add, [S["orecv"][d].astype(F32) * shares[d] for d in range(Z)]
    )
    out_t = (merged / total).astype(BF16)
    S["ot"][...] = out_t
    log_norm = top + jnp.log(total)
    S["stats"][z, 0:1, :] = log_norm

    spread(S["ts"], nt(S["routing"][...], jnp.concatenate([out_t, out_t], axis=1)))
    for i in range(X):
        exchange_send(token_exchange, i)
        if i == X // 2 - 1:
            advance_grads()
    drains.append(lambda: exchange_drain(token_exchange))

    def pair(buf, block):
        return jnp.concatenate([buf[2 * block], buf[2 * block + 1]], axis=1)

    def columns(block):
        return pl.ds(pl.multiple_of(block * (2 * HD), 2 * HD), 2 * HD)

    order = [0]
    for k in range(1, Y // 2 + 1):
        order += sorted({k, Y - k})

    for copy in weights_in:
        copy.wait()
    while grad_hops:
        advance_grads()
    for n, d in enumerate(order):
        sib_wait(S["grads"], "gsib", d)
        block = lax.rem(y + d, Y)
        term = nt(pair(S["grads"], block), S["wout"][:, columns(block)])
        S["thr"][...] = term if n == 0 else S["thr"][...] + term

    token_ring = feature_ring(S["toks"], "ytk")
    drains.append(token_ring.drain)
    drains.append(lambda: sib_drain(S["toks"], "tsib"))
    ring_from_exchange(token_exchange, S["toks"], token_ring, "tsib")

    def pre_term(d):
        sib_wait(S["toks"], "tsib", d)
        block = lax.rem(y + d, Y)
        term = nn(pair(S["toks"], block), S["win"][columns(block), :])
        S["pre"][...] = term if d == 0 else S["pre"][...] + term

    for k in range(1, y_half + 2):
        if k <= y_half:
            ring_hop(token_ring, S["toks"], "tsib", k)
        for d in neighbours(k - 1, Y):
            pre_term(d)

    pre = S["pre"][...]
    logistic = 1.0 / (1.0 + jnp.exp(-pre))
    S["hg"][...] = (S["thr"][...] * logistic * (1.0 + pre * (1.0 - logistic))).astype(BF16)

    def partner_copy(distance):
        block = lax.rem(y + distance, Y)
        return remote(S["sb"].at[block], S["rb"].at[block], S["sem_psib_s"].at[distance],
                      S["sem_psib_r"].at[distance], sibling)

    far_first = order[::-1]
    for d in far_first:
        block = lax.rem(y + d, Y)
        share = nt(S["hg"][...], S["win"][columns(block), :]).astype(BF16)
        first, second = share[:, :HD], share[:, HD:]
        S["pb"][block] = jnp.where(c == 0, first, second)
        S["sb"][block] = jnp.where(c == 0, second, first)
        partner_copy(d).start()
        drains.append(partner_copy(d).wait_send)

    S["hid"][...] = jnp.transpose(pre * logistic).astype(BF16)
    half = y_half

    def hops(direction, chunk):
        return half if (chunk < X // 2) == (direction == 0) else half - 1

    def ring_copy(direction, chunk, h):
        i = X * h + chunk
        ends = ("_rs", "_rr") if direction == 0 else ("_ls", "_lr")
        neighbour = ydev(lax.rem(y + 1, Y)) if direction == 0 else ydev(lax.rem(y + Y - 1, Y))
        return remote(S["rs_stage"].at[direction, i], S["rs_recv"].at[direction, i],
                      S["sem_rs" + ends[0]].at[i], S["sem_rs" + ends[1]].at[i], neighbour)

    def own_part(block, chunk):
        span = part_rows(chunk)
        return S["pb"][block, span, :].astype(F32) + S["rb"][block, span, :].astype(F32)

    lanes = [(0, i) for i in range(X)] + [(1, (i + X // 2) % X) for i in range(X)]
    lanes = [lane for both in zip(lanes[:X], lanes[X:]) for lane in both]

    weight_work = [("out", d) for d in order] + [("in", d) for d in order]

    def some_weight_work(count):
        for _ in range(min(count, len(weight_work))):
            which, d = weight_work.pop(0)
            block = lax.rem(y + d, Y)
            if which == "out":
                dwo_ref[0, :, columns(block)] = nn(S["hid"][...], pair(S["grads"], block)).astype(BF16)
            else:
                dwi_ref[0, columns(block), :] = tn(pair(S["toks"], block), S["hg"][...]).astype(BF16)

    waited = set()

    def need_partner(distance):
        if distance not in waited:
            waited.add(distance)
            partner_copy(distance).wait_recv()

    per_hop = -(-2 * Y // half)
    for h in range(half):
        for direction, chunk in lanes:
            total_hops = hops(direction, chunk)
            if h >= total_hops:
                continue
            distance = total_hops - h if direction == 0 else Y - (total_hops - h)
            need_partner(distance)
            value = own_part(lax.rem(y + distance, Y), chunk)
            if h > 0:
                ring_copy(direction, chunk, h - 1).wait_recv()
                value = value + S["rs_recv"][direction, X * (h - 1) + chunk].astype(F32)
            S["rs_stage"][direction, X * h + chunk] = value.astype(BF16)
            ring_copy(direction, chunk, h).start()
            drains.append(ring_copy(direction, chunk, h).wait_send)
        some_weight_work(per_hop)
    need_partner(0)
    for chunk in range(X):
        value = own_part(y, chunk)
        for direction in range(2):
            last = hops(direction, chunk) - 1
            if last >= 0:
                ring_copy(direction, chunk, last).wait_recv()
                value = value + S["rs_recv"][direction, X * last + chunk].astype(F32)
        padded = nn(S["compt"][...], value.astype(BF16)).reshape(Z, PAD, HD)
        S["bs"][pl.ds(row_of(chunk) * Z, Z)] = padded.astype(BF16)
        exchange_send(back_exchange, (X - chunk) % X)
    drains.append(lambda: exchange_drain(back_exchange))
    some_weight_work(2 * Y)
    for i in range(X):
        exchange_wait(back_exchange, i)
    returned = S["br"][...].astype(F32).reshape(RP, HD).astype(BF16)
    combined = tn(returned, S["routing"][...])
    grad_t = (S["ogt"][...] + combined[:, :BL] + combined[:, BL:]).astype(BF16).astype(F32)
    delta = jnp.sum(grad_t * S["ot"][...].astype(F32), axis=0, keepdims=True)
    S["stats"][z, 1:2, :] = delta
    S["gb"][z] = jnp.transpose(grad_t).astype(BF16)

    g_ring = GatherRing(
        Z, 2, z, zdev, lambda b, p: S["gb"].at[b, pl.ds(p * (BL // 2), BL // 2), :],
        [S["sem_g_rs"], S["sem_g_rr"], S["sem_g_ls"], S["sem_g_lr"]],
    )

    def stats_copy(d, block):
        ref = S["stats"].at[block]
        return remote(ref, ref, S["sem_st_s"].at[d], S["sem_st_r"].at[d], zdev(lax.rem(z + d, Z)))

    for part in range(2):
        g_ring.start(part)
    drains.append(g_ring.drain)
    for d in range(1, Z):
        stats_copy(d, z).start()
        drains.append(stats_copy(d, z).wait_send)

    def dq_copy(d):
        return remote(S["dqsend"].at[d], S["dqrecv"].at[d], S["sem_dq_s"].at[d], S["sem_dq_r"].at[d],
                      zdev(lax.rem(z + d, Z)))

    def backward(d):
        j = lax.rem(z + d, Z)
        queries, grads = S["qb"][j], S["gb"][j]
        norm, dlt = S["stats"][j, 0:1, :], S["stats"][j, 1:2, :]
        dq = 0.0
        for r, offset, mask in pieces(d, j):
            p = jnp.exp(scores_of(r, offset, mask, queries) - norm)
            dv = nn(p.astype(BF16), grads)
            ds = (p * (nt(S["v3"][r], grads) - dlt)).astype(BF16)
            dk = nn(ds, queries)
            dq = dq + nn(S["kt3"][r], ds)
            if d == 0:
                S["dv3"][r], S["dk3"][r] = dv, dk
            else:
                S["dv3"][r] = S["dv3"][r] + dv
                S["dk3"][r] = S["dk3"][r] + dk
        dq = dq * scale
        if d == 0:
            S["dqown"][...] = dq
        else:
            S["dqsend"][d] = dq.astype(BF16)
            dq_copy(d).start()
            drains.append(dq_copy(d).wait_send)

    for k in range(1, z_half + 2):
        if k <= z_half:
            for part in range(2):
                g_ring.step(k, part)
        for d in neighbours(k - 1, Z):
            if d:
                stats_copy(Z - d, lax.rem(z + d, Z)).wait_recv()
            backward(d)

    dkv_copies = []
    for hop in (1, 2):
        S["dksend"][hop - 1] = (S["dk3"][hop] * scale).astype(BF16)
        S["dvsend"][hop - 1] = S["dv3"][hop].astype(BF16)
        for which, name in enumerate(("dk", "dv")):
            i = 2 * (hop - 1) + which
            copy = remote(S[name + "send"].at[hop - 1], S[name + "recv"].at[hop - 1],
                          S["sem_dkv_s"].at[i], S["sem_dkv_r"].at[i], xdev(x + X - hop))
            copy.start()
            dkv_copies.append(copy)
            drains.append(copy.wait_send)

    dq = S["dqown"][...]
    for d in range(1, Z):
        dq_copy(d).wait_recv()
        dq = dq + S["dqrecv"][d].astype(F32)
    dq_ref[...] = jnp.transpose(dq).astype(BF16)
    for copy in dkv_copies:
        copy.wait_recv()
    dk_ref[...] = (
        S["dk3"][0] * scale + S["dkrecv"][0].astype(F32) + S["dkrecv"][1].astype(F32)
    ).astype(BF16)
    dv_ref[...] = (
        S["dv3"][0] + S["dvrecv"][0].astype(F32) + S["dvrecv"][1].astype(F32)
    ).astype(BF16)

    for f in drains:
        f()


def hand_over(*refs):
    sems = refs[10]
    copies = [pltpu.make_async_copy(refs[i], refs[5 + i], sems.at[i]) for i in range(5)]
    for copy in copies:
        copy.start()
    for copy in copies:
        copy.wait()


def per_device(
    queries,
    key_rows,
    value_rows,
    out_grad,
    expert_ids,
    gate_values,
    alibi_slope,
    expert_in,
    expert_out,
):
    E, N = lax.axis_size("seq"), lax.axis_size("exp")
    Y, Z = N // 2, WCH // 2
    BL = queries.shape[0]
    D, FL = expert_in.shape[1:]
    CAP = 5 * BL // (2 * E)
    scratch = scratch_table(E, Y, Z, BL, D, FL, CAP)
    vmem = pl.BlockSpec(memory_space=pltpu.VMEM)
    smem = pl.BlockSpec(memory_space=pltpu.SMEM)
    hbm = pl.BlockSpec(memory_space=pl.ANY)
    kept = [queries.shape] * 3 + [expert_in.shape, expert_out.shape]
    outs = pl.pallas_call(
        functools.partial(body, list(scratch), E, Y, Z, CAP),
        out_shape=tuple(pltpu.VMEM(out, BF16) for out in kept),
        in_specs=[vmem] * 6 + [smem] + [hbm] * 2,
        out_specs=(vmem,) * 5,
        scratch_shapes=list(scratch.values()),
        compiler_params=pltpu.CompilerParams(
            collective_id=0, has_side_effects=True, vmem_limit_bytes=56 * 2**20
        ),
    )(
        queries,
        key_rows,
        value_rows,
        out_grad,
        expert_ids.T,
        gate_values.T,
        alibi_slope,
        expert_in,
        expert_out,
    )
    return pl.pallas_call(
        hand_over,
        out_shape=tuple(jax.ShapeDtypeStruct(out, BF16) for out in kept),
        in_specs=[vmem] * 5,
        out_specs=(hbm,) * 5,
        scratch_shapes=[pltpu.SemaphoreType.DMA((5,))],
    )(*(pltpu.with_memory_space_constraint(out, pltpu.VMEM) for out in outs))


def solution(mesh):
    return jax.shard_map(
        per_device,
        mesh=mesh,
        in_specs=(
            P("seq", "exp"),
            P("seq", "exp"),
            P("seq", "exp"),
            P("seq", "exp"),
            P("seq", None),
            P("seq", None),
            P("exp"),
            P("seq", None, "exp"),
            P("seq", "exp", None),
        ),
        out_specs=(
            P("seq", "exp"),
            P("seq", "exp"),
            P("seq", "exp"),
            P("seq", None, "exp"),
            P("seq", "exp", None),
        ),
        check_vma=False,
    )
```

```python
import functools

import jax
import jax.numpy as jnp
from jax import lax
from jax.experimental import pallas as pl
from jax.experimental.pallas import tpu as pltpu
from jax.sharding import PartitionSpec as P

HD = 128
WCH = 16
PAD = 24
F32 = jnp.float32
BF16 = jnp.bfloat16
MESH = pl.DeviceIdType.MESH
NEG = -1.0e30


def nt(a, b):
    return lax.dot_general(a, b, (((1,), (1,)), ((), ())), preferred_element_type=F32)


def nn(a, b):
    return lax.dot_general(a, b, (((1,), (0,)), ((), ())), preferred_element_type=F32)


def tn(a, b):
    return lax.dot_general(a, b, (((0,), (0,)), ((), ())), preferred_element_type=F32)


def transposed(a):
    return jnp.transpose(a.astype(F32)).astype(BF16)


def remote(src, dst, send_sem, recv_sem, device):
    return pltpu.make_async_remote_copy(
        src_ref=src,
        dst_ref=dst,
        send_sem=send_sem,
        recv_sem=recv_sem,
        device_id=device,
        device_id_type=MESH,
    )


class GatherRing:
    def __init__(self, count, parts, me, device_of, view, sems):
        self.n, self.parts, self.me, self.view = count, parts, me, view
        self.half = count // 2
        self.right = device_of(lax.rem(me + 1, count))
        self.left = device_of(lax.rem(me + count - 1, count))
        self.sems = sems

    def block(self, direction, hops):
        return lax.rem(self.me + (self.n - hops if direction == 0 else hops), self.n)

    def sends(self, direction, k, part):
        return k < self.half - 1 or (k == self.half - 1 and self.ahead(direction, part))

    def ahead(self, direction, part):
        return (part < self.parts // 2) == (direction == 0)

    def copy(self, direction, k, part, hops):
        ref = self.view(self.block(direction, hops), part)
        i = self.parts * k + part
        return remote(
            ref,
            ref,
            self.sems[2 * direction].at[i],
            self.sems[2 * direction + 1].at[i],
            self.right if direction == 0 else self.left,
        )

    def start(self, part):
        for direction in range(2):
            if self.sends(direction, 0, part):
                self.copy(direction, 0, part, 0).start()

    def step(self, k, part):
        for direction in range(2):
            if not self.sends(direction, k - 1, part):
                continue
            self.copy(direction, k - 1, part, k).wait_recv()
            if self.sends(direction, k, part):
                self.copy(direction, k, part, k).start()

    def drain(self):
        for k in range(self.half):
            for part in range(self.parts):
                for direction in range(2):
                    if self.sends(direction, k, part):
                        self.copy(direction, k, part, k).wait_send()


def scratch_table(E, Y, Z, BL, D, FL, CAP):
    R, RP, hz, hy, X = E * CAP, E * PAD, max(Z // 2, 1), max(Y // 2, 1), E // Z
    table = dict(
        k3=((3, BL, HD), BF16),
        v3=((3, BL, HD), BF16),
        kt3=((3, HD, BL), BF16),
        vt3=((3, HD, BL), BF16),
        qb=((Z, BL, HD), BF16),
        relay=((BL, HD), BF16),
        gb=((Z, BL, HD), BF16),
        cb=((BL, BL), F32),
        osend=((Z, HD, BL), BF16),
        orecv=((Z, HD, BL), BF16),
        lsend=((Z, 1, BL), F32),
        lrecv=((Z, 1, BL), F32),
        stats=((Z, 2, BL), F32),
        ot=((HD, BL), BF16),
        ogt=((HD, BL), F32),
        routing=((RP, 2 * BL), BF16),
        comp=((R // X, RP // X), BF16),
        compt=((RP // X, R // X), BF16),
        gs=((E, PAD, HD), BF16),
        gr=((E, PAD, HD), BF16),
        ts=((E, PAD, HD), BF16),
        tr=((E, PAD, HD), BF16),
        bs=((E, PAD, HD), BF16),
        br=((E, PAD, HD), BF16),
        grads=((2 * Y, R, HD), BF16),
        toks=((2 * Y, R, HD), BF16),
        win=((D, FL), BF16),
        wout=((FL, D), BF16),
        thr=((R, FL), F32),
        pre=((R, FL), F32),
        hid=((FL, R), BF16),
        hg=((R, FL), BF16),
        pb=((Y, R, HD), BF16),
        sb=((Y, R, HD), BF16),
        rb=((Y, R, HD), BF16),
        rs_stage=((2, X * hy, R // X, HD), BF16),
        rs_recv=((2, X * hy, R // X, HD), BF16),
        dk3=((3, BL, HD), F32),
        dv3=((3, BL, HD), F32),
        dksend=((2, BL, HD), BF16),
        dvsend=((2, BL, HD), BF16),
        dkrecv=((2, BL, HD), BF16),
        dvrecv=((2, BL, HD), BF16),
        dqsend=((Z, HD, BL), BF16),
        dqrecv=((Z, HD, BL), BF16),
        dqown=((HD, BL), F32),
    )
    shapes = {name: pltpu.VMEM(shape, dtype) for name, (shape, dtype) in table.items()}
    counts = dict(
        kv_s=4, kv_r=4, o_s=Z, o_r=Z, l_s=Z, l_r=Z, st_s=Z, st_r=Z, dq_s=Z, dq_r=Z, dkv_s=4, dkv_r=4,
        ga_s=E, ga_r=E, ta_s=E, ta_r=E, ba_s=E, ba_r=E, w=2, own=3, re_s=2, re_r=2,
        gsib_s=X * Y, gsib_r=X * Y, tsib_s=X * Y, tsib_r=X * Y, psib_s=Y, psib_r=Y,
    )
    for ring, half in (("q", 2 * hz), ("g", 2 * hz), ("ygr", X * hy), ("ytk", X * hy), ("rs", X * hy)):
        for end in ("_rs", "_rr", "_ls", "_lr"):
            counts[ring + end] = half
    for name, count in counts.items():
        shapes["sem_" + name] = pltpu.SemaphoreType.DMA((count,))
    shapes["columns_in"] = pltpu.SemaphoreType.REGULAR
    return shapes


def body(names, E, Y, Z, CAP, *refs):
    (q_ref, k_ref, v_ref, og_ref, ids_ref, gates_ref, slope_ref, win_ref, wout_ref,
     dq_ref, dk_ref, dv_ref, dwi_ref, dwo_ref) = refs[:14]
    S = dict(zip(names, refs[14:]))
    BL, FL = q_ref.shape[0], win_ref.shape[2]
    X, R, RP, D = E // Z, E * CAP, E * PAD, 2 * Y * HD
    scale = HD ** (-0.5)
    s, e = lax.axis_index("seq"), lax.axis_index("exp")
    x, z = lax.div(s, Z), lax.rem(s, Z)
    y, c = lax.div(e, 2), lax.rem(e, 2)
    sibling = (s, 2 * y + 1 - c)

    def zdev(j):
        return (x * Z + j, e)

    def xdev(i):
        return (lax.rem(i, X) * Z + z, e)

    def ydev(j):
        return (s, 2 * j + c)

    drains = []
    barrier = pltpu.get_barrier_semaphore()
    near = [zdev(lax.rem(z + d, Z)) for d in range(1, Z)] + [xdev(x + d) for d in range(1, X)]
    near += [ydev(lax.rem(y + 1, Y)), ydev(lax.rem(y + Y - 1, Y)), sibling]
    for device in near:
        pl.semaphore_signal(barrier, inc=1, device_id=device, device_id_type=MESH)

    own_rows = [
        pltpu.make_async_copy(q_ref, S["qb"].at[z], S["sem_own"].at[0]),
        pltpu.make_async_copy(k_ref, S["k3"].at[0], S["sem_own"].at[1]),
        pltpu.make_async_copy(v_ref, S["v3"].at[0], S["sem_own"].at[2]),
    ]
    for copy in own_rows:
        copy.start()
    weights_in = [
        pltpu.make_async_copy(win_ref.at[0], S["win"], S["sem_w"].at[0]),
        pltpu.make_async_copy(wout_ref.at[0], S["wout"], S["sem_w"].at[1]),
    ]
    for copy in weights_in:
        copy.start()
    for copy in own_rows:
        copy.wait()
    pl.semaphore_wait(barrier, len(near))

    q_ring = GatherRing(
        Z, 2, z, zdev, lambda b, p: S["qb"].at[b, pl.ds(p * (BL // 2), BL // 2), :],
        [S["sem_q_rs"], S["sem_q_rr"], S["sem_q_ls"], S["sem_q_lr"]],
    )
    for part in range(2):
        q_ring.start(part)
    drains.append(q_ring.drain)
    kv_copies = []
    for hop in (1, 2):
        for which, (own, buf) in enumerate((("k3", "k3"), ("v3", "v3"))):
            i = 2 * (hop - 1) + which
            if i == 3 and X == 4:
                continue
            copy = remote(
                S[own].at[0], S[buf].at[hop], S["sem_kv_s"].at[i], S["sem_kv_r"].at[i],
                xdev(x + hop),
            )
            copy.start()
            kv_copies.append(copy)
            drains.append(copy.wait_send)

    def relay_copy(leg):
        return remote(
            S["v3"].at[0] if leg == 0 else S["relay"],
            S["relay"] if leg == 0 else S["v3"].at[2],
            S["sem_re_s"].at[leg], S["sem_re_r"].at[leg], xdev(x + X - 1),
        )

    if X == 4:
        relay_copy(0).start()

    y_half, z_half = Y // 2, Z // 2
    query_hops = list(range(1, z_half + 1))

    def take_queries(upto):
        while query_hops and query_hops[0] <= upto:
            k = query_hops.pop(0)
            for part in range(2):
                q_ring.step(k, part)

    for d in range(1, X):
        pl.semaphore_signal(
            S["columns_in"], inc=1, device_id=xdev(x + d), device_id_type=MESH
        )

    flat = jnp.concatenate([ids_ref[0:1, :], ids_ref[1:2, :]], axis=1)
    hot = lax.broadcasted_iota(jnp.int32, (E, 2 * BL), 0) == flat
    hot_f = jnp.where(hot, 1.0, 0.0)
    upper = lax.broadcasted_iota(jnp.int32, (2 * BL, 2 * BL), 0) < lax.broadcasted_iota(
        jnp.int32, (2 * BL, 2 * BL), 1
    )
    before = nn(hot_f.astype(BF16), jnp.where(upper, 1.0, 0.0).astype(BF16))
    position = jnp.sum(before * hot_f, axis=0, keepdims=True)
    slot = jnp.where(position < CAP, flat * PAD + position.astype(jnp.int32), -1)
    S["routing"][...] = jnp.where(
        lax.broadcasted_iota(jnp.int32, (RP, 2 * BL), 0) == slot, 1.0, 0.0
    ).astype(BF16)
    ogt = jnp.transpose(og_ref[...].astype(F32))
    S["ogt"][...] = ogt
    scaled = jnp.concatenate([ogt * gates_ref[0:1, :], ogt * gates_ref[1:2, :]], axis=1)
    def spread(send, value):
        send[...] = value.reshape(E, PAD, HD).astype(BF16)

    def row_of(i):
        return lax.rem(x + i, X)

    def exchange_copy(exchange, i, j, outward):
        send, recv, sems = exchange
        k = i * Z + j
        if outward:
            peer = lax.rem(x + X - i, X) * Z + lax.rem(z + j, Z)
            return remote(send.at[peer], recv.at[s], S[sems + "_s"].at[k], S[sems + "_r"].at[k], (peer, e))
        peer = row_of(i) * Z + lax.rem(z + Z - j, Z)
        return remote(send.at[peer], recv.at[peer], S[sems + "_s"].at[k], S[sems + "_r"].at[k], (peer, e))

    def each_peer(i, act):
        def go(j, carry):
            act(j)
            return carry

        lax.fori_loop(1 if i == 0 else 0, Z, go, 0)

    def exchange_send(exchange, i):
        if i == 0:
            exchange[1][s] = exchange[0][s]
        each_peer(i, lambda j: exchange_copy(exchange, i, j, True).start())

    def exchange_wait(exchange, i):
        each_peer(i, lambda j: exchange_copy(exchange, i, j, False).wait_recv())

    def exchange_drain(exchange):
        for i in range(X):
            each_peer(i, lambda j: exchange_copy(exchange, i, j, True).wait_send())

    grad_exchange = (S["gs"], S["gr"], "sem_ga")
    token_exchange = (S["ts"], S["tr"], "sem_ta")
    back_exchange = (S["bs"], S["br"], "sem_ba")
    spread(S["gs"], nt(S["routing"][...], scaled.astype(BF16)))
    take_queries(1)
    if X == 4:
        relay_copy(0).wait_recv()
        relay_copy(1).start()
        drains += [relay_copy(0).wait_send, relay_copy(1).wait_send]
    pl.semaphore_wait(S["columns_in"], X - 1)
    for i in range(X):
        exchange_send(grad_exchange, i)
    drains.append(lambda: exchange_drain(grad_exchange))
    take_queries(2)

    per_part, padded_part = R // X, RP // X

    def packed_of(index):
        block = (index * (65536 // PAD + 1)) >> 16
        inner = index - block * PAD
        return jnp.where(inner < CAP, block * CAP + inner, -1)

    S["comp"][...] = jnp.where(
        lax.broadcasted_iota(jnp.int32, (per_part, padded_part), 0)
        == packed_of(lax.broadcasted_iota(jnp.int32, (per_part, padded_part), 1)),
        1.0,
        0.0,
    ).astype(BF16)
    S["compt"][...] = jnp.where(
        packed_of(lax.broadcasted_iota(jnp.int32, (padded_part, per_part), 0))
        == lax.broadcasted_iota(jnp.int32, (padded_part, per_part), 1),
        1.0,
        0.0,
    ).astype(BF16)

    def part_rows(i):
        align = 16 if per_part % 16 == 0 else 1
        return pl.ds(pl.multiple_of(row_of(i) * per_part, align), per_part)

    def pack(exchange, buf, i):
        part = exchange[1][pl.ds(row_of(i) * Z, Z)].astype(F32).reshape(padded_part, HD)
        buf[e, part_rows(i), :] = nn(S["comp"][...], part.astype(BF16)).astype(BF16)

    slope = slope_ref[0]
    S["cb"][...] = lax.broadcasted_iota(jnp.int32, (BL, BL), 0).astype(F32) * slope
    causal = lax.broadcasted_iota(jnp.int32, (BL, BL), 0) <= lax.broadcasted_iota(
        jnp.int32, (BL, BL), 1
    )

    def pieces(d, j):
        def offset(r):
            distance = ((j - z) * BL).astype(F32) + float(r * Z * BL)
            return jnp.where(x >= r, 0.0, NEG) - slope * distance

        if d == 0:
            return [(0, offset(0), causal), (1, offset(1), None), (2, offset(2), ~causal)]
        r = jnp.where(j > z, 0, 2)
        near = jnp.where(j > z, offset(0), offset(2))
        return [(r, near, None), (1, offset(1), None)]

    def scores_of(r, offset, mask, queries):
        raw = nt(S["k3"][r], queries) * scale + (S["cb"][...] + offset)
        return raw if mask is None else jnp.where(mask, raw, NEG)

    def forward(d):
        j = lax.rem(z + d, Z)
        queries = S["qb"][j]
        parts = pieces(d, j)
        scores = [scores_of(r, offset, mask, queries) for r, offset, mask in parts]
        top = functools.reduce(
            jnp.maximum, [jnp.max(t, axis=0, keepdims=True) for t in scores]
        )
        total, out = 0.0, 0.0
        for (r, _, _), t in zip(parts, scores):
            p = jnp.exp(t - top)
            total = total + jnp.sum(p, axis=0, keepdims=True)
            out = out + nn(S["vt3"][r], p.astype(BF16))
        out = (out / total).astype(BF16)
        log_norm = top + jnp.log(total)
        if d == 0:
            S["orecv"][0] = out
            S["lrecv"][0] = log_norm
            return
        S["osend"][d] = out
        S["lsend"][d] = log_norm
        out_copy(d).start()
        norm_copy(d).start()
        drains.append(out_copy(d).wait_send)
        drains.append(norm_copy(d).wait_send)

    def out_copy(d):
        return remote(S["osend"].at[d], S["orecv"].at[d], S["sem_o_s"].at[d], S["sem_o_r"].at[d],
                      zdev(lax.rem(z + d, Z)))

    def norm_copy(d):
        return remote(S["lsend"].at[d], S["lrecv"].at[d], S["sem_l_s"].at[d], S["sem_l_r"].at[d],
                      zdev(lax.rem(z + d, Z)))

    def feature_view(buf, block, core, part):
        return buf.at[2 * block + core, part_rows(part), :]

    def feature_ring(buf, ring):
        return GatherRing(
            Y, X, y, ydev, lambda b, p: feature_view(buf, b, c, p),
            [S["sem_" + ring + end] for end in ("_rs", "_rr", "_ls", "_lr")],
        )

    def sib_copies(buf, sib, distance, core):
        block = 2 * lax.rem(y + distance, Y) + core
        refs = [buf.at[block]]
        if distance == y_half:
            refs = [buf.at[block, part_rows(part), :] for part in range(X)]
        return [
            remote(ref, ref, S["sem_" + sib + "_s"].at[distance + Y * n],
                   S["sem_" + sib + "_r"].at[distance + Y * n], sibling)
            for n, ref in enumerate(refs)
        ]

    def sib_send(buf, sib, k):
        for distance in neighbours(k, Y):
            for copy in sib_copies(buf, sib, distance, c):
                copy.start()

    def sib_wait(buf, sib, distance):
        for copy in sib_copies(buf, sib, distance, 1 - c):
            copy.wait_recv()

    def sib_drain(buf, sib):
        for distance in range(Y):
            for copy in sib_copies(buf, sib, distance, c):
                copy.wait_send()

    def ring_hop(ring, buf, sib, k):
        for part in range(X):
            ring.step(k, part)
            if k == y_half:
                sib_copies(buf, sib, k, c)[part].start()
        if k < y_half:
            sib_send(buf, sib, k)

    def neighbours(k, n):
        return [0] if k == 0 else sorted({k, n - k})

    def ring_from_exchange(exchange, buf, ring, sib):
        for i in range(X):
            exchange_wait(exchange, i)
            pack(exchange, buf, i)
            ring.start(i)
        sib_send(buf, sib, 0)

    grad_ring = feature_ring(S["grads"], "ygr")
    drains.append(grad_ring.drain)
    drains.append(lambda: sib_drain(S["grads"], "gsib"))
    grad_hops = list(range(y_half + 1))

    def advance_grads():
        if not grad_hops:
            return
        k = grad_hops.pop(0)
        if k == 0:
            ring_from_exchange(grad_exchange, S["grads"], grad_ring, "gsib")
        else:
            ring_hop(grad_ring, S["grads"], "gsib", k)

    S["kt3"][0] = transposed(S["k3"][0])
    S["vt3"][0] = transposed(S["v3"][0])
    for copy in kv_copies:
        copy.wait_recv()
    if X == 4:
        relay_copy(1).wait_recv()
    for r in (1, 2):
        S["kt3"][r] = transposed(S["k3"][r])
        S["vt3"][r] = transposed(S["v3"][r])
    forward(0)
    take_queries(3)
    for k in range(1, z_half + 1):
        if k == z_half:
            take_queries(k)
        for d in neighbours(k, Z):
            forward(d)
        if k != 2:
            advance_grads()

    for d in range(1, Z):
        out_copy(d).wait_recv()
        norm_copy(d).wait_recv()
    norms = [S["lrecv"][d][0:1, :] for d in range(Z)]
    top = functools.reduce(jnp.maximum, norms)
    shares = [jnp.exp(t - top) for t in norms]
    total = functools.reduce(jnp.add, shares)
    merged = functools.reduce(
        jnp.add, [S["orecv"][d].astype(F32) * shares[d] for d in range(Z)]
    )
    out_t = (merged / total).astype(BF16)
    S["ot"][...] = out_t
    log_norm = top + jnp.log(total)
    S["stats"][z, 0:1, :] = log_norm

    spread(S["ts"], nt(S["routing"][...], jnp.concatenate([out_t, out_t], axis=1)))
    for i in range(X):
        exchange_send(token_exchange, i)
        if i == X // 2 - 1:
            advance_grads()
    drains.append(lambda: exchange_drain(token_exchange))

    def pair(buf, block):
        return jnp.concatenate([buf[2 * block], buf[2 * block + 1]], axis=1)

    def columns(block):
        return pl.ds(pl.multiple_of(block * (2 * HD), 2 * HD), 2 * HD)

    order = [0]
    for k in range(1, Y // 2 + 1):
        order += sorted({k, Y - k})

    for copy in weights_in:
        copy.wait()
    while grad_hops:
        advance_grads()
    for n, d in enumerate(order):
        sib_wait(S["grads"], "gsib", d)
        block = lax.rem(y + d, Y)
        term = nt(pair(S["grads"], block), S["wout"][:, columns(block)])
        S["thr"][...] = term if n == 0 else S["thr"][...] + term

    token_ring = feature_ring(S["toks"], "ytk")
    drains.append(token_ring.drain)
    drains.append(lambda: sib_drain(S["toks"], "tsib"))
    ring_from_exchange(token_exchange, S["toks"], token_ring, "tsib")

    def pre_term(d):
        sib_wait(S["toks"], "tsib", d)
        block = lax.rem(y + d, Y)
        term = nn(pair(S["toks"], block), S["win"][columns(block), :])
        S["pre"][...] = term if d == 0 else S["pre"][...] + term

    for k in range(1, y_half + 2):
        if k <= y_half:
            ring_hop(token_ring, S["toks"], "tsib", k)
        for d in neighbours(k - 1, Y):
            pre_term(d)

    pre = S["pre"][...]
    logistic = 1.0 / (1.0 + jnp.exp(-pre))
    S["hg"][...] = (S["thr"][...] * logistic * (1.0 + pre * (1.0 - logistic))).astype(BF16)

    def partner_copy(distance):
        block = lax.rem(y + distance, Y)
        return remote(S["sb"].at[block], S["rb"].at[block], S["sem_psib_s"].at[distance],
                      S["sem_psib_r"].at[distance], sibling)

    far_first = order[::-1]
    for d in far_first:
        block = lax.rem(y + d, Y)
        share = nt(S["hg"][...], S["win"][columns(block), :]).astype(BF16)
        first, second = share[:, :HD], share[:, HD:]
        S["pb"][block] = jnp.where(c == 0, first, second)
        S["sb"][block] = jnp.where(c == 0, second, first)
        partner_copy(d).start()
        drains.append(partner_copy(d).wait_send)

    S["hid"][...] = jnp.transpose(pre * logistic).astype(BF16)
    half = y_half

    def hops(direction, chunk):
        return half if (chunk < X // 2) == (direction == 0) else half - 1

    def ring_copy(direction, chunk, h):
        i = X * h + chunk
        ends = ("_rs", "_rr") if direction == 0 else ("_ls", "_lr")
        neighbour = ydev(lax.rem(y + 1, Y)) if direction == 0 else ydev(lax.rem(y + Y - 1, Y))
        return remote(S["rs_stage"].at[direction, i], S["rs_recv"].at[direction, i],
                      S["sem_rs" + ends[0]].at[i], S["sem_rs" + ends[1]].at[i], neighbour)

    def own_part(block, chunk):
        span = part_rows(chunk)
        return S["pb"][block, span, :].astype(F32) + S["rb"][block, span, :].astype(F32)

    lanes = [(0, i) for i in range(X)] + [(1, (i + X // 2) % X) for i in range(X)]
    lanes = [lane for both in zip(lanes[:X], lanes[X:]) for lane in both]

    weight_work = [("out", d) for d in order] + [("in", d) for d in order]

    def some_weight_work(count):
        for _ in range(min(count, len(weight_work))):
            which, d = weight_work.pop(0)
            block = lax.rem(y + d, Y)
            if which == "out":
                dwo_ref[0, :, columns(block)] = nn(S["hid"][...], pair(S["grads"], block)).astype(BF16)
            else:
                dwi_ref[0, columns(block), :] = tn(pair(S["toks"], block), S["hg"][...]).astype(BF16)

    waited = set()

    def need_partner(distance):
        if distance not in waited:
            waited.add(distance)
            partner_copy(distance).wait_recv()

    per_hop = -(-2 * Y // half)
    for h in range(half):
        for direction, chunk in lanes:
            total_hops = hops(direction, chunk)
            if h >= total_hops:
                continue
            distance = total_hops - h if direction == 0 else Y - (total_hops - h)
            need_partner(distance)
            value = own_part(lax.rem(y + distance, Y), chunk)
            if h > 0:
                ring_copy(direction, chunk, h - 1).wait_recv()
                value = value + S["rs_recv"][direction, X * (h - 1) + chunk].astype(F32)
            S["rs_stage"][direction, X * h + chunk] = value.astype(BF16)
            ring_copy(direction, chunk, h).start()
            drains.append(ring_copy(direction, chunk, h).wait_send)
        some_weight_work(per_hop)
    need_partner(0)
    for chunk in range(X):
        value = own_part(y, chunk)
        for direction in range(2):
            last = hops(direction, chunk) - 1
            if last >= 0:
                ring_copy(direction, chunk, last).wait_recv()
                value = value + S["rs_recv"][direction, X * last + chunk].astype(F32)
        padded = nn(S["compt"][...], value.astype(BF16)).reshape(Z, PAD, HD)
        S["bs"][pl.ds(row_of(chunk) * Z, Z)] = padded.astype(BF16)
        exchange_send(back_exchange, (X - chunk) % X)
    drains.append(lambda: exchange_drain(back_exchange))
    some_weight_work(2 * Y)
    for i in range(X):
        exchange_wait(back_exchange, i)
    returned = S["br"][...].astype(F32).reshape(RP, HD).astype(BF16)
    combined = tn(returned, S["routing"][...])
    grad_t = (S["ogt"][...] + combined[:, :BL] + combined[:, BL:]).astype(BF16).astype(F32)
    delta = jnp.sum(grad_t * S["ot"][...].astype(F32), axis=0, keepdims=True)
    S["stats"][z, 1:2, :] = delta
    S["gb"][z] = jnp.transpose(grad_t).astype(BF16)

    g_ring = GatherRing(
        Z, 2, z, zdev, lambda b, p: S["gb"].at[b, pl.ds(p * (BL // 2), BL // 2), :],
        [S["sem_g_rs"], S["sem_g_rr"], S["sem_g_ls"], S["sem_g_lr"]],
    )

    def stats_copy(d, block):
        ref = S["stats"].at[block]
        return remote(ref, ref, S["sem_st_s"].at[d], S["sem_st_r"].at[d], zdev(lax.rem(z + d, Z)))

    for part in range(2):
        g_ring.start(part)
    drains.append(g_ring.drain)
    for d in range(1, Z):
        stats_copy(d, z).start()
        drains.append(stats_copy(d, z).wait_send)

    def dq_copy(d):
        return remote(S["dqsend"].at[d], S["dqrecv"].at[d], S["sem_dq_s"].at[d], S["sem_dq_r"].at[d],
                      zdev(lax.rem(z + d, Z)))

    def backward(d):
        j = lax.rem(z + d, Z)
        queries, grads = S["qb"][j], S["gb"][j]
        norm, dlt = S["stats"][j, 0:1, :], S["stats"][j, 1:2, :]
        dq = 0.0
        for r, offset, mask in pieces(d, j):
            p = jnp.exp(scores_of(r, offset, mask, queries) - norm)
            dv = nn(p.astype(BF16), grads)
            ds = (p * (nt(S["v3"][r], grads) - dlt)).astype(BF16)
            dk = nn(ds, queries)
            dq = dq + nn(S["kt3"][r], ds)
            if d == 0:
                S["dv3"][r], S["dk3"][r] = dv, dk
            else:
                S["dv3"][r] = S["dv3"][r] + dv
                S["dk3"][r] = S["dk3"][r] + dk
        dq = dq * scale
        if d == 0:
            S["dqown"][...] = dq
        else:
            S["dqsend"][d] = dq.astype(BF16)
            dq_copy(d).start()
            drains.append(dq_copy(d).wait_send)

    for k in range(1, z_half + 2):
        if k <= z_half:
            for part in range(2):
                g_ring.step(k, part)
        for d in neighbours(k - 1, Z):
            if d:
                stats_copy(Z - d, lax.rem(z + d, Z)).wait_recv()
            backward(d)

    dkv_copies = []
    for hop in (1, 2):
        S["dksend"][hop - 1] = (S["dk3"][hop] * scale).astype(BF16)
        S["dvsend"][hop - 1] = S["dv3"][hop].astype(BF16)
        for which, name in enumerate(("dk", "dv")):
            i = 2 * (hop - 1) + which
            copy = remote(S[name + "send"].at[hop - 1], S[name + "recv"].at[hop - 1],
                          S["sem_dkv_s"].at[i], S["sem_dkv_r"].at[i], xdev(x + X - hop))
            copy.start()
            dkv_copies.append(copy)
            drains.append(copy.wait_send)

    dq = S["dqown"][...]
    for d in range(1, Z):
        dq_copy(d).wait_recv()
        dq = dq + S["dqrecv"][d].astype(F32)
    dq_ref[...] = jnp.transpose(dq).astype(BF16)
    for copy in dkv_copies:
        copy.wait_recv()
    dk_ref[...] = (
        S["dk3"][0] * scale + S["dkrecv"][0].astype(F32) + S["dkrecv"][1].astype(F32)
    ).astype(BF16)
    dv_ref[...] = (
        S["dv3"][0] + S["dvrecv"][0].astype(F32) + S["dvrecv"][1].astype(F32)
    ).astype(BF16)

    for f in drains:
        f()


def hand_over(*refs):
    sems = refs[10]
    copies = [pltpu.make_async_copy(refs[i], refs[5 + i], sems.at[i]) for i in range(5)]
    for copy in copies:
        copy.start()
    for copy in copies:
        copy.wait()


def per_device(
    queries,
    key_rows,
    value_rows,
    out_grad,
    expert_ids,
    gate_values,
    alibi_slope,
    expert_in,
    expert_out,
):
    E, N = lax.axis_size("seq"), lax.axis_size("exp")
    Y, Z = N // 2, WCH // 2
    BL = queries.shape[0]
    D, FL = expert_in.shape[1:]
    CAP = 5 * BL // (2 * E)
    scratch = scratch_table(E, Y, Z, BL, D, FL, CAP)
    vmem = pl.BlockSpec(memory_space=pltpu.VMEM)
    smem = pl.BlockSpec(memory_space=pltpu.SMEM)
    hbm = pl.BlockSpec(memory_space=pl.ANY)
    kept = [queries.shape] * 3 + [expert_in.shape, expert_out.shape]
    outs = pl.pallas_call(
        functools.partial(body, list(scratch), E, Y, Z, CAP),
        out_shape=tuple(pltpu.VMEM(out, BF16) for out in kept),
        in_specs=[hbm] * 3 + [vmem] * 3 + [smem] + [hbm] * 2,
        out_specs=(vmem,) * 5,
        scratch_shapes=list(scratch.values()),
        compiler_params=pltpu.CompilerParams(
            collective_id=0, has_side_effects=True, vmem_limit_bytes=56 * 2**20
        ),
    )(
        queries,
        key_rows,
        value_rows,
        out_grad,
        expert_ids.T,
        gate_values.T,
        alibi_slope,
        expert_in,
        expert_out,
    )
    return pl.pallas_call(
        hand_over,
        out_shape=tuple(jax.ShapeDtypeStruct(out, BF16) for out in kept),
        in_specs=[vmem] * 5,
        out_specs=(hbm,) * 5,
        scratch_shapes=[pltpu.SemaphoreType.DMA((5,))],
    )(*(pltpu.with_memory_space_constraint(out, pltpu.VMEM) for out in outs))


def solution(mesh):
    return jax.shard_map(
        per_device,
        mesh=mesh,
        in_specs=(
            P("seq", "exp"),
            P("seq", "exp"),
            P("seq", "exp"),
            P("seq", "exp"),
            P("seq", None),
            P("seq", None),
            P("exp"),
            P("seq", None, "exp"),
            P("seq", "exp", None),
        ),
        out_specs=(
            P("seq", "exp"),
            P("seq", "exp"),
            P("seq", "exp"),
            P("seq", None, "exp"),
            P("seq", "exp", None),
        ),
        check_vma=False,
    )
```
